32 devices in a mesh: dp: 8 (over z, y), mp: 4 (over x, core).
Axes of the slice: x: 2, y: 2, z: 4, core: 2. Of those that a mesh axis runs over, the one named last changes fastest.
Arguments:
- activations: bfloat16 [4096, 8192], P(('dp', 'mp')), may hold values from -6 to 6
- grad_out: bfloat16 [4096, 28672], P('dp', 'mp'), may hold values from -0.25 to 0.25
- basis: bfloat16 [8192, 256], P('dp'), may hold values from -0.0625 to 0.0625
- first_moment: float32 [28672, 256], P(('mp', 'dp')), may hold values from -3 to 3
- second_moment: float32 [28672, 256], P(('mp', 'dp')), may hold values from 0.01 to 0.5
Outputs:
- update: bfloat16 [8192, 28672], P('dp', 'mp')
- first_new: float32 [28672, 256], P(('mp', 'dp'))
- second_new: float32 [28672, 256], P(('mp', 'dp'))
The draws below stay inside these ranges and needn't reach their ends.
All inputs are finite; a program needn't handle non-finite values.
Results may differ from the reference program's by a relative error of at most 0.0069.
Values may be sent and summed in bfloat16 or wider, within the bound.
No kernel may reach another device: no remote copies, remote signals or barrier semaphores. Data moves between devices by JAX's collectives and lax.ppermute only.
A program may use at most 128 MiB of HBM per device.

```python
import math
import jax
import jax.numpy as jnp
from jax import lax

D = 8192
FF = 28672
R = 256
STEP = 1000
TOKENS = 4096


def strengthened(drawn, own_key, source, target, shards_of, factor):
    def block_of(position):
        return (jnp.arange(drawn.shape[position]) // (drawn.shape[position] // shards_of)).reshape((-1,) + (1,) * (drawn.ndim - 1 - position))

    first = jax.random.permutation(own_key, shards_of)[block_of(target)]
    other_side = (block_of(target) + shards_of // 2) % shards_of
    return jnp.where((block_of(source) == first) | (block_of(source) == other_side), factor * drawn, drawn)


def block_levels(rng, extent, shards, smallest, high):
    gain, own = 1.0, jax.random.fold_in(rng, 6)
    for dim, blocks in shards:
        draws = jnp.exp(jax.random.uniform(jax.random.fold_in(own, dim), (blocks,), jnp.float32, smallest / len(shards), high / len(shards)))
        gain = gain * jnp.repeat(draws, extent[dim] // blocks).reshape([-1 if axis == dim else 1 for axis in range(len(extent))])
    return gain


def normal_values(own_key, shape, width, bound, cuts=(), held_as=jnp.bfloat16):
    drawn = jax.random.normal(own_key, shape, jnp.float32) * width
    if len(cuts) > 0:
        drawn = block_levels(own_key, shape, cuts, -0.22, 0.18) * drawn
    return jnp.clip(drawn, min=-bound, max=bound).astype(held_as)


def gaussian_with(own_key, extent, scale, reach, cuts, heavy, held_as=jnp.bfloat16):
    values = scale * jax.random.normal(own_key, extent, jnp.float32)
    if cuts:
        values = values * block_levels(own_key, extent, cuts, -0.22, 0.18)
    return jnp.clip(strengthened(values, jax.random.fold_in(own_key, 3), *heavy), -reach, reach).astype(held_as)


def setup_inputs(seed: int = 0) -> dict:
    keys = jax.random.split(jax.random.key(seed), 6)
    activations = normal_values(keys[0], (TOKENS, D), 1.0, 6.0, ((0, 32),))
    grad_out = gaussian_with(keys[1], (TOKENS, FF), (TOKENS // 4) ** -0.5, 0.25, ((0, 8), (1, 4)), (0, 1, 8, 2.0))
    basis = normal_values(keys[2], (D, R), D ** -0.5, 0.0625, ((0, 8),))
    first_moment = normal_values(keys[3], (FF, R), 0.5, 3.0, ((0, 32),), jnp.float32)
    second_moment = jnp.clip(jnp.exp(math.log(0.5) - 3.912023 * jax.random.uniform(keys[4], (FF, R), jnp.float32) ** block_levels(keys[4], (FF, R), ((0, 32),), -0.2, 0.2)), 0.01, 0.5)
    return {"activations": activations, "grad_out": grad_out, "basis": basis, "first_moment": first_moment, "second_moment": second_moment}


beta_first = 0.9
beta_second = 0.999
adam_eps = 1e-08

def reference(activations, grad_out, basis, first_moment, second_moment):
    coords = jnp.dot(activations, basis, preferred_element_type=jnp.float32).astype(jnp.bfloat16)
    projected = lax.dot_general(grad_out, coords, (((0,), (0,)), ((), ())), preferred_element_type=jnp.float32)
    first_new = beta_first * first_moment + (1.0 - beta_first) * projected
    second_new = beta_second * second_moment + (1.0 - beta_second) * projected * projected
    corr_first = 1.0 - beta_first ** STEP
    corr_second = 1.0 - beta_second ** STEP
    direction = (first_new / corr_first / (jnp.sqrt(second_new / corr_second) + adam_eps)).astype(jnp.bfloat16)
    update = lax.dot_general(basis, direction, (((1,), (1,)), ((), ())), preferred_element_type=jnp.float32).astype(jnp.bfloat16)
    return (update, first_new, second_new)
```

```python
import functools

import jax
import jax.numpy as jnp
import numpy as np
from jax import lax
from jax.experimental import pallas as pl
from jax.experimental.pallas import tpu as pltpu
from jax.sharding import PartitionSpec as P

STEP = 1000


beta_first = 0.9
beta_second = 0.999
adam_eps = 1e-08

STREAMS = 2
LONGEST_RING = 16


def adam(projected, first_moment, second_moment):
    first_new = beta_first * first_moment + (1.0 - beta_first) * projected
    second_new = beta_second * second_moment + (1.0 - beta_second) * projected * projected
    corr_first = 1.0 - beta_first**STEP
    corr_second = 1.0 - beta_second**STEP
    direction = (first_new / corr_first / (jnp.sqrt(second_new / corr_second) + adam_eps)).astype(
        jnp.bfloat16
    )
    return first_new, second_new, direction


def with_collectives(activations, grad_out, basis, first_moment, second_moment):
    own_coords = jnp.dot(
        activations, lax.all_gather(basis, "dp", axis=0, tiled=True), preferred_element_type=jnp.float32
    ).astype(jnp.bfloat16)
    coords = lax.all_gather(own_coords, "mp", axis=0, tiled=True)
    projected = lax.psum_scatter(
        lax.dot_general(
            grad_out, coords, (((0,), (0,)), ((), ())), preferred_element_type=jnp.float32
        ),
        "dp",
        scatter_dimension=0,
        tiled=True,
    )
    first_new, second_new, direction = adam(projected, first_moment, second_moment)
    update = lax.dot_general(
        basis,
        lax.all_gather(direction, "dp", axis=0, tiled=True),
        (((1,), (1,)), ((), ())),
        preferred_element_type=jnp.float32,
    ).astype(jnp.bfloat16)
    return (update, first_new, second_new)


def whole(shape):
    return pl.BlockSpec(shape, lambda *_: (0,) * len(shape))


def add_coords(offsets, activations, total, pieces, out_dtype):
    rows, width = activations.shape[0], pieces[0].shape[1]
    held = () if total is None else (total,)

    def kernel(at, act, *refs):
        out = refs[-1]
        acc = refs[0][...] if held else jnp.zeros((rows, width), jnp.float32)
        for k, piece in enumerate(refs[len(held) : -1]):
            depth = piece.shape[0]
            block = act[:, pl.ds(pl.multiple_of(at[k], 128), depth)]
            acc += jnp.dot(block, piece[...], preferred_element_type=jnp.float32)
        out[...] = acc.astype(out.dtype)

    return pl.pallas_call(
        kernel,
        out_shape=jax.ShapeDtypeStruct((rows, width), out_dtype),
        grid_spec=pltpu.PrefetchScalarGridSpec(
            num_scalar_prefetch=1,
            grid=(1,),
            in_specs=[whole(a.shape) for a in (activations, *held, *pieces)],
            out_specs=whole((rows, width)),
        ),
        name="add_coords",
    )(offsets, activations, *held, *pieces)


def contract_tokens(grad, coords):
    return lax.dot_general(grad, coords, (((0,), (0,)), ((), ())), preferred_element_type=jnp.float32)


def first_partials(ids, grad_out, coords, n, cols):
    tokens, width = coords.shape

    def kernel(ids_ref, grad, coord, top, bottom):
        part = contract_tokens(grad[...], coord[...]).astype(jnp.bfloat16)
        top[...] = part[: cols // 2]
        bottom[...] = part[cols // 2 :]

    half = jax.ShapeDtypeStruct((cols // 2, width), jnp.bfloat16)
    return pl.pallas_call(
        kernel,
        out_shape=(half, half),
        grid_spec=pltpu.PrefetchScalarGridSpec(
            num_scalar_prefetch=1,
            grid=(1,),
            in_specs=[
                pl.BlockSpec((tokens, cols), lambda g, ids: (0, ids[n // 2])),
                whole(coords.shape),
            ],
            out_specs=(whole(half.shape), whole(half.shape)),
        ),
        name="first_partials",
    )(ids, grad_out, coords)


def next_partials(ids, grad_out, coords, came_up, came_down, n, cols, away):
    tokens, width = coords.shape
    rows = came_up.shape[0]

    def kernel(ids_ref, grad, coord, in_up, in_down, up, down):
        part = contract_tokens(grad[...], coord[...])

        @pl.when(pl.program_id(0) == 0)
        def _():
            up[:rows] = (part[:rows] + in_up[...].astype(jnp.float32)).astype(jnp.bfloat16)
            if rows < cols:
                up[rows:] = part[rows:].astype(jnp.bfloat16)

        @pl.when(pl.program_id(0) == 1)
        def _():
            down[cols - rows :] = (
                part[cols - rows :] + in_down[...].astype(jnp.float32)
            ).astype(jnp.bfloat16)
            if rows < cols:
                down[: cols - rows] = part[: cols - rows].astype(jnp.bfloat16)

    full = jax.ShapeDtypeStruct((cols, width), jnp.bfloat16)
    return pl.pallas_call(
        kernel,
        out_shape=(full, full),
        grid_spec=pltpu.PrefetchScalarGridSpec(
            num_scalar_prefetch=1,
            grid=(2,),
            in_specs=[
                pl.BlockSpec(
                    (tokens, cols), lambda g, ids: (0, jnp.where(g == 0, ids[away], ids[n - away]))
                ),
                whole(coords.shape),
                whole(came_up.shape),
                whole(came_down.shape),
            ],
            out_specs=(whole(full.shape), whole(full.shape)),
        ),
        name="next_partials",
    )(ids, grad_out, coords, came_up, came_down)


def own_rows(ids, grad_out, coords, came_up, came_down, first_moment, second_moment, earlier, s, cols):
    tokens, width = coords.shape
    held = () if earlier is None else earlier

    def kernel(ids_ref, grad, coord, in_up, in_down, first, second, *refs):
        first_new, second_new, direction = refs[len(held) :]
        projected = (
            contract_tokens(grad[...], coord[...])
            + in_up[...].astype(jnp.float32)
            + in_down[...].astype(jnp.float32)
        )
        first_new[...], second_new[...], direction[...] = adam(projected, first[...], second[...])

    part = pl.BlockSpec((cols, width), lambda g, ids: (0, s))
    moment = jax.ShapeDtypeStruct(first_moment.shape, jnp.float32)
    return pl.pallas_call(
        kernel,
        out_shape=(moment, moment, jax.ShapeDtypeStruct((cols, width), jnp.bfloat16)),
        grid_spec=pltpu.PrefetchScalarGridSpec(
            num_scalar_prefetch=1,
            grid=(1,),
            in_specs=[
                pl.BlockSpec((tokens, cols), lambda g, ids: (0, ids[0])),
                whole(coords.shape),
                whole(came_up.shape),
                whole(came_down.shape),
                part,
                part,
                *[pl.BlockSpec(memory_space=pl.ANY)] * len(held),
            ],
            out_specs=(part, part, whole((cols, width))),
        ),
        input_output_aliases={7 + k: k for k in range(len(held))},
        name="own_rows",
    )(ids, grad_out, coords, came_up, came_down, first_moment, second_moment, *held)


def write_update(ids, basis, chunks, places, update, all_columns):
    depth, rank = basis.shape
    cols = sum(row[0].shape[0] for row in chunks[0])
    flat = [stream for chunk in chunks for row in chunk for stream in row]
    held = () if update is None else (update,)
    tile = depth // 2

    def kernel(ids_ref, base, *refs):
        out = refs[-1]
        left = list(refs[: len(flat)])
        for g, chunk in enumerate(chunks):
            rows = [[left.pop(0) for _ in row] for row in chunk]

            @pl.when(pl.program_id(0) == g)
            def _(rows=rows):
                at = 0
                for row in rows:
                    size, width = row[0].shape
                    total = None
                    for s, stream in enumerate(row):
                        product = lax.dot_general(
                            base[:, s * width : (s + 1) * width],
                            stream[...],
                            (((1,), (1,)), ((), ())),
                            preferred_element_type=jnp.float32,
                        )
                        total = product if total is None else total + product
                    out[:, at : at + size] = total.astype(out.dtype)
                    at += size

    def place(g, r, ids):
        at = ids[places[0]]
        for k in range(1, len(places)):
            at = jnp.where(g == k, ids[places[k]], at)
        return (r, at)

    return pl.pallas_call(
        kernel,
        out_shape=jax.ShapeDtypeStruct((depth, all_columns), jnp.bfloat16),
        grid_spec=pltpu.PrefetchScalarGridSpec(
            num_scalar_prefetch=1,
            grid=(len(chunks), depth // tile),
            in_specs=[
                pl.BlockSpec((tile, rank), lambda g, r, ids: (r, 0)),
                *[whole(a.shape) for a in flat],
                *[pl.BlockSpec(memory_space=pl.ANY)] * len(held),
            ],
            out_specs=pl.BlockSpec((tile, cols), place),
        ),
        input_output_aliases={2 + len(flat): 0} if held else {},
        name="write_update",
    )(ids, basis, *flat, *held)


def on_ring(n, m, activations, grad_out, basis, first_moment, second_moment):
    order = [*range(0, n, 2), *range(n - 1, 0, -2)]
    upward = [(order[k], order[(k + 1) % n]) for k in range(n)]
    downward = [(b, a) for a, b in upward]
    partner = [(k, k ^ 1) for k in range(m)]
    up = functools.partial(lax.ppermute, axis_name="dp", perm=upward)
    down = functools.partial(lax.ppermute, axis_name="dp", perm=downward)

    around = np.zeros((n, n), np.int32)
    for place, index in enumerate(order):
        around[index] = [order[(place + away) % n] for away in range(n)]
    ids = jnp.asarray(around)[lax.axis_index("dp")]
    mine = lax.axis_index("mp")
    side = mine % 2

    depth, rank = basis.shape
    tokens = activations.shape[0]
    width = rank // STREAMS
    all_columns = grad_out.shape[1]
    cols = all_columns // n
    half = n // 2
    streams = range(STREAMS)

    part = depth // 2
    sent_up = [None] * STREAMS
    sent_down = [None] * STREAMS
    total = [None] * STREAMS
    for s in streams:
        own = basis[:, s * width : (s + 1) * width]
        sent_up[s] = sent_down[s] = lax.dynamic_slice(own, (side * part, 0), (part, width))
        total[s] = add_coords(ids[:1] * depth, activations, None, [own], jnp.float32)
    for k in range(1, half + 1):
        for s in streams:
            if k == half:
                sent_up[s], sent_down[s] = sent_up[s][: part // 2], sent_down[s][part // 2 :]
            sent_up[s], sent_down[s] = up(sent_up[s]), down(sent_down[s])
            pieces = [sent_up[s], sent_down[s]]
            pieces += [lax.ppermute(a, "mp", partner) for a in pieces]
            low = part // 2 if k == half else 0
            at = jnp.stack(
                [
                    ids[n - k] * depth + side * part,
                    ids[k] * depth + side * part + low,
                    ids[n - k] * depth + (1 - side) * part,
                    ids[k] * depth + (1 - side) * part + low,
                ]
            )
            total[s] = add_coords(
                at, activations, total[s], pieces, jnp.bfloat16 if k == half else jnp.float32
            )

    coords = [None] * STREAMS
    for s in streams:
        parts = [total[s]]
        for k in range(1, m):
            parts.append(lax.ppermute(total[s], "mp", [(a, (a + k) % m) for a in range(m)]))
        turned = [parts[-k % m] for k in range(m)]
        coords[s] = lax.dynamic_slice(
            jnp.concatenate(turned + turned), ((m - mine) % m * tokens, 0), (m * tokens, width)
        )

    for s in streams:
        top, bottom = first_partials(ids, grad_out, coords[s], n, cols)
        sent_up[s], sent_down[s] = up(top), down(bottom)
    for away in range(half - 1, 0, -1):
        for s in streams:
            to_up, to_down = next_partials(
                ids, grad_out, coords[s], sent_up[s], sent_down[s], n, cols, away
            )
            sent_up[s], sent_down[s] = up(to_up), down(to_down)
    moments = None
    direction = [None] * STREAMS
    for s in streams:
        *moments, direction[s] = own_rows(
            ids, grad_out, coords[s], sent_up[s], sent_down[s], first_moment, second_moment, moments, s, cols
        )
    first_new, second_new = moments

    sent_up, sent_down = list(direction), list(direction)
    update = write_update(ids, basis, [[direction]], [0], None, all_columns)
    for k in range(1, half):
        for s in streams:
            sent_up[s], sent_down[s] = up(sent_up[s]), down(sent_down[s])
        update = write_update(
            ids, basis, [[list(sent_up)], [list(sent_down)]], [n - k, k], update, all_columns
        )
    for s in streams:
        sent_up[s], sent_down[s] = up(sent_up[s][: cols // 2]), down(sent_down[s][cols // 2 :])
    update = write_update(ids, basis, [[sent_up, sent_down]], [half], update, all_columns)
    return (update, first_new, second_new)


def solution(mesh):
    n, m = mesh.shape["dp"], mesh.shape["mp"]
    ring = 4 <= n <= LONGEST_RING and n % 2 == 0 and m % 2 == 0
    placed = (
        P(("dp", "mp"), None),
        P("dp", "mp"),
        P("dp", None),
        P(("mp", "dp"), None),
        P(("mp", "dp"), None),
    )
    return jax.shard_map(
        functools.partial(on_ring, n, m) if ring else with_collectives,
        mesh=mesh,
        in_specs=placed,
        out_specs=(P("dp", "mp"), P(("mp", "dp"), None), P(("mp", "dp"), None)),
        check_vma=False,
    )
```

```python
import functools

import jax
import jax.numpy as jnp
import numpy as np
from jax import lax
from jax.experimental import pallas as pl
from jax.experimental.pallas import tpu as pltpu
from jax.sharding import PartitionSpec as P

STEP = 1000


beta_first = 0.9
beta_second = 0.999
adam_eps = 1e-08

STREAMS = 2
LONGEST_RING = 16
SCRATCH_BYTES = 12 << 20


def adam(projected, first_moment, second_moment):
    first_new = beta_first * first_moment + (1.0 - beta_first) * projected
    second_new = beta_second * second_moment + (1.0 - beta_second) * projected * projected
    corr_first = 1.0 - beta_first**STEP
    corr_second = 1.0 - beta_second**STEP
    direction = (first_new / corr_first / (jnp.sqrt(second_new / corr_second) + adam_eps)).astype(
        jnp.bfloat16
    )
    return first_new, second_new, direction


def with_collectives(activations, grad_out, basis, first_moment, second_moment):
    own_coords = jnp.dot(
        activations, lax.all_gather(basis, "dp", axis=0, tiled=True), preferred_element_type=jnp.float32
    ).astype(jnp.bfloat16)
    coords = lax.all_gather(own_coords, "mp", axis=0, tiled=True)
    projected = lax.psum_scatter(
        lax.dot_general(
            grad_out, coords, (((0,), (0,)), ((), ())), preferred_element_type=jnp.float32
        ),
        "dp",
        scatter_dimension=0,
        tiled=True,
    )
    first_new, second_new, direction = adam(projected, first_moment, second_moment)
    update = lax.dot_general(
        basis,
        lax.all_gather(direction, "dp", axis=0, tiled=True),
        (((1,), (1,)), ((), ())),
        preferred_element_type=jnp.float32,
    ).astype(jnp.bfloat16)
    return (update, first_new, second_new)


def on_chip():
    return pl.BlockSpec(memory_space=pltpu.VMEM)


def scalars():
    return pl.BlockSpec(memory_space=pltpu.SMEM)


def kept_on_chip(arrays):
    return [pltpu.with_memory_space_constraint(a, pltpu.VMEM) for a in arrays]


def split_columns(me, activations, n):
    tokens, features = activations.shape
    part = features // n // 2

    def kernel(me_ref, own, other, kept, sent):
        kept[...] = own[...]
        sent[...] = other[...]

    half = jax.ShapeDtypeStruct((tokens, features // 2), activations.dtype)
    return pl.pallas_call(
        kernel,
        out_shape=(half, half),
        grid_spec=pltpu.PrefetchScalarGridSpec(
            num_scalar_prefetch=1,
            grid=(n,),
            in_specs=[
                pl.BlockSpec((tokens, part), lambda j, me: (0, 2 * j + me[0] % 2)),
                pl.BlockSpec((tokens, part), lambda j, me: (0, 2 * j + 1 - me[0] % 2)),
            ],
            out_specs=(pl.BlockSpec((tokens, part), lambda j, me: (0, j)),) * 2,
        ),
        compiler_params=pltpu.CompilerParams(vmem_limit_bytes=SCRATCH_BYTES),
        name="split_columns",
    )(me, activations, activations)


def add_coords(ids, me, kept, came, total, pieces, depth):
    tokens, width = kept.shape[0], pieces[0][0].shape[1]
    held = () if total is None else (total,)
    arrays = [piece for piece, _, _ in pieces]

    def kernel(ids_ref, me_ref, *refs):
        out = refs[-1]
        side = me_ref[0] % 2
        refs_of = refs[2 + len(held) : -1]
        for act, place in ((refs[0], side), (refs[1], 1 - side)):
            rows = pl.ds(pl.multiple_of(place * tokens, tokens), tokens)
            acc = refs[2][rows] if held else jnp.zeros((tokens, width), jnp.float32)
            for ref, (_, away, low) in zip(refs_of, pieces, strict=True):
                start = pl.multiple_of(ids_ref[away] * depth + low, 128)
                acc += jnp.dot(
                    act[:, pl.ds(start, ref.shape[0])], ref[...], preferred_element_type=jnp.float32
                )
            out[rows] = acc

    return pl.pallas_call(
        kernel,
        out_shape=pltpu.VMEM((2 * tokens, width), jnp.float32),
        in_specs=[scalars(), scalars(), *[on_chip()] * (2 + len(held) + len(arrays))],
        out_specs=on_chip(),
        cost_estimate=pl.CostEstimate(
            flops=4 * tokens * width * sum(a.shape[0] for a in arrays), transcendentals=0, bytes_accessed=4 << 20
        ),
        compiler_params=pltpu.CompilerParams(vmem_limit_bytes=SCRATCH_BYTES),
        name="add_coords",
    )(ids, me, *kept_on_chip([kept, came, *held, *arrays]))


def contract_tokens(grad, coords):
    return lax.dot_general(grad, coords, (((0,), (0,)), ((), ())), preferred_element_type=jnp.float32)


def first_partials(ids, me, grad_out, parts, n):
    group, width = parts[0].shape
    tokens, all_columns = grad_out.shape
    cols = all_columns // n
    groups = tokens // group

    def kernel(ids_ref, me_ref, grad, *refs):
        coords, top, bottom = refs[len(parts) :]
        for k, ref in enumerate(refs[: len(parts)]):
            at = lax.rem(me_ref[0] // 2 + groups - k, groups)
            coords[pl.ds(pl.multiple_of(at * group, group), group)] = ref[...]
        column = pl.multiple_of(ids_ref[n // 2] * cols, 128)
        part = contract_tokens(grad[:, pl.ds(column, cols)], coords[...]).astype(jnp.bfloat16)
        top[...] = part[: cols // 2]
        bottom[...] = part[cols // 2 :]

    half = pltpu.VMEM((cols // 2, width), jnp.bfloat16)
    return pl.pallas_call(
        kernel,
        out_shape=(pltpu.VMEM((tokens, width), jnp.bfloat16), half, half),
        in_specs=[scalars(), scalars(), *[on_chip()] * (1 + len(parts))],
        out_specs=(on_chip(),) * 3,
        cost_estimate=pl.CostEstimate(
            flops=2 * tokens * cols * width, transcendentals=0, bytes_accessed=4 << 20
        ),
        compiler_params=pltpu.CompilerParams(vmem_limit_bytes=SCRATCH_BYTES),
        name="first_partials",
    )(ids, me, *kept_on_chip([grad_out, *parts]))


def next_partials(ids, grad_out, coords, came_up, came_down, n, away):
    tokens, width = coords.shape
    cols = grad_out.shape[1] // n
    rows = came_up.shape[0]

    def kernel(ids_ref, grad, coord, in_up, in_down, up, down):
        column = pl.multiple_of(ids_ref[away] * cols, 128)
        part = contract_tokens(grad[:, pl.ds(column, cols)], coord[...])
        up[:rows] = (part[:rows] + in_up[...].astype(jnp.float32)).astype(jnp.bfloat16)
        if rows < cols:
            up[rows:] = part[rows:].astype(jnp.bfloat16)
        column = pl.multiple_of(ids_ref[n - away] * cols, 128)
        part = contract_tokens(grad[:, pl.ds(column, cols)], coord[...])
        rest = cols - rows
        down[rest:] = (part[rest:] + in_down[...].astype(jnp.float32)).astype(jnp.bfloat16)
        if rest:
            down[:rest] = part[:rest].astype(jnp.bfloat16)

    full = pltpu.VMEM((cols, width), jnp.bfloat16)
    return pl.pallas_call(
        kernel,
        out_shape=(full, full),
        in_specs=[scalars(), *[on_chip()] * 4],
        out_specs=(on_chip(),) * 2,
        cost_estimate=pl.CostEstimate(
            flops=4 * tokens * cols * width, transcendentals=0, bytes_accessed=4 << 20
        ),
        compiler_params=pltpu.CompilerParams(vmem_limit_bytes=SCRATCH_BYTES),
        name="next_partials",
    )(ids, *kept_on_chip([grad_out, coords, came_up, came_down]))


def own_direction(ids, grad_out, coords, came_up, came_down, first_moment, second_moment, s, n):
    tokens, width = coords.shape
    cols = grad_out.shape[1] // n

    def kernel(ids_ref, grad, coord, in_up, in_down, first, second, projected, direction):
        column = pl.multiple_of(ids_ref[0] * cols, 128)
        total = (
            contract_tokens(grad[:, pl.ds(column, cols)], coord[...])
            + in_up[...].astype(jnp.float32)
            + in_down[...].astype(jnp.float32)
        )
        projected[...] = total
        mine = slice(s * width, (s + 1) * width)
        direction[...] = adam(total, first[:, mine], second[:, mine])[2]

    return pl.pallas_call(
        kernel,
        out_shape=(
            pltpu.VMEM((cols, width), jnp.float32),
            pltpu.VMEM((cols, width), jnp.bfloat16),
        ),
        in_specs=[scalars(), *[on_chip()] * 6],
        out_specs=(on_chip(),) * 2,
        cost_estimate=pl.CostEstimate(
            flops=2 * tokens * cols * width, transcendentals=0, bytes_accessed=4 << 20
        ),
        compiler_params=pltpu.CompilerParams(vmem_limit_bytes=SCRATCH_BYTES),
        name="own_direction",
    )(ids, *kept_on_chip([grad_out, coords, came_up, came_down, first_moment, second_moment]))


def new_moments(projected, first_moment, second_moment):
    width = projected[0].shape[1]
    rows = first_moment.shape[0]
    tile = rows // 2
    block = pl.BlockSpec((tile, first_moment.shape[1]), lambda r: (r, 0))

    def kernel(*refs):
        first, second, first_new, second_new = refs[len(projected) :]
        for s, ref in enumerate(refs[: len(projected)]):
            mine = slice(s * width, (s + 1) * width)
            at = pl.ds(pl.multiple_of(pl.program_id(0) * tile, tile), tile)
            first_new[:, mine], second_new[:, mine], _ = adam(ref[at], first[at, mine], second[at, mine])

    return pl.pallas_call(
        kernel,
        out_shape=(jax.ShapeDtypeStruct(first_moment.shape, jnp.float32),) * 2,
        grid=(rows // tile,),
        in_specs=[on_chip()] * (len(projected) + 2),
        out_specs=(block, block),
        cost_estimate=pl.CostEstimate(flops=0, transcendentals=0, bytes_accessed=6 << 20),
        compiler_params=pltpu.CompilerParams(vmem_limit_bytes=SCRATCH_BYTES),
        name="new_moments",
    )(*kept_on_chip([*projected, first_moment, second_moment]))


def write_update(ids, basis, chunks, places, update, all_columns):
    depth, rank = basis.shape
    cols = sum(row[0].shape[0] for row in chunks[0])
    flat = [stream for chunk in chunks for row in chunk for stream in row]
    held = () if update is None else (update,)
    tile = depth // 2

    def kernel(ids_ref, base, *refs):
        out = refs[-1]
        left = list(refs[: len(flat)])
        lines = pl.ds(pl.multiple_of(pl.program_id(1) * tile, tile), tile)
        for g, chunk in enumerate(chunks):
            rows = [[left.pop(0) for _ in row] for row in chunk]

            @pl.when(pl.program_id(0) == g)
            def _(rows=rows):
                whole = jnp.concatenate(
                    [jnp.concatenate([stream[...] for stream in row], axis=1) for row in rows], axis=0
                )
                out[...] = lax.dot_general(
                    base[lines], whole, (((1,), (1,)), ((), ())), preferred_element_type=jnp.float32
                ).astype(out.dtype)

    def place(g, r, ids):
        at = ids[places[0]]
        for k in range(1, len(places)):
            at = jnp.where(g == k, ids[places[k]], at)
        return (r, at)

    return pl.pallas_call(
        kernel,
        out_shape=jax.ShapeDtypeStruct((depth, all_columns), jnp.bfloat16),
        grid_spec=pltpu.PrefetchScalarGridSpec(
            num_scalar_prefetch=1,
            grid=(len(chunks), depth // tile),
            in_specs=[
                *[on_chip()] * (1 + len(flat)),
                *[pl.BlockSpec(memory_space=pl.ANY)] * len(held),
            ],
            out_specs=pl.BlockSpec((tile, cols), place),
        ),
        input_output_aliases={2 + len(flat): 0} if held else {},
        cost_estimate=pl.CostEstimate(
            flops=2 * depth * cols * rank * len(chunks),
            transcendentals=0,
            bytes_accessed=2 * depth * cols * len(chunks),
        ),
        compiler_params=pltpu.CompilerParams(vmem_limit_bytes=SCRATCH_BYTES),
        name="write_update",
    )(ids, *kept_on_chip([basis, *flat]), *held)


def on_ring(n, m, activations, grad_out, basis, first_moment, second_moment):
    order = [*range(0, n, 2), *range(n - 1, 0, -2)]
    upward = [(order[k], order[(k + 1) % n]) for k in range(n)]
    downward = [(b, a) for a, b in upward]
    up = functools.partial(lax.ppermute, axis_name="dp", perm=upward)
    down = functools.partial(lax.ppermute, axis_name="dp", perm=downward)
    swap = functools.partial(lax.ppermute, axis_name="mp", perm=[(k, k ^ 1) for k in range(m)])

    around = np.zeros((n, n), np.int32)
    for place, index in enumerate(order):
        around[index] = [order[(place + away) % n] for away in range(n)]
    ids = jnp.asarray(around)[lax.axis_index("dp")]
    me = lax.axis_index("mp").reshape(1)

    depth, rank = basis.shape
    width = rank // STREAMS
    all_columns = grad_out.shape[1]
    cols = all_columns // n
    half = n // 2
    streams = range(STREAMS)

    part = depth // 2
    own = lax.dynamic_slice(basis, (me[0] % 2 * part, 0), (part, rank))
    own = [own[:, s * width : (s + 1) * width] for s in streams]
    sent_up, sent_down = list(own), list(own)
    pieces = [[(own[s], 0, 0)] for s in streams]
    kept, sent = split_columns(me, activations, n)
    came = swap(sent)
    total = [None] * STREAMS
    for k in range(1, half + 1):
        for s in streams:
            low = 0
            if k == half:
                low = part // 2
                sent_up[s], sent_down[s] = sent_up[s][:low], sent_down[s][low:]
            sent_up[s], sent_down[s] = up(sent_up[s]), down(sent_down[s])
            pieces[s] += [(sent_up[s], n - k, 0), (sent_down[s], k, low)]
            if k >= half - 1:
                total[s] = add_coords(ids, me, kept, came, total[s], pieces[s], part)
                pieces[s] = []

    parts = [None] * STREAMS
    for s in streams:
        pair = (total[s] + swap(total[s])).astype(jnp.bfloat16)
        parts[s] = [pair] + [
            lax.ppermute(pair, "mp", [(a, (a + k) % m) for a in range(m)]) for k in range(2, m, 2)
        ]

    coords = [None] * STREAMS
    for s in streams:
        coords[s], top, bottom = first_partials(ids, me, grad_out, parts[s], n)
        sent_up[s], sent_down[s] = up(top), down(bottom)
    for away in range(half - 1, 0, -1):
        for s in streams:
            to_up, to_down = next_partials(ids, grad_out, coords[s], sent_up[s], sent_down[s], n, away)
            sent_up[s], sent_down[s] = up(to_up), down(to_down)
    projected = [None] * STREAMS
    direction = [None] * STREAMS
    for s in streams:
        projected[s], direction[s] = own_direction(
            ids, grad_out, coords[s], sent_up[s], sent_down[s], first_moment, second_moment, s, n
        )

    sent_up, sent_down = list(direction), list(direction)
    update = write_update(ids, basis, [[direction]], [0], None, all_columns)
    first_new, second_new = new_moments(projected, first_moment, second_moment)
    for k in range(1, half):
        for s in streams:
            sent_up[s], sent_down[s] = up(sent_up[s]), down(sent_down[s])
        sent_up[0], update = lax.optimization_barrier((sent_up[0], update))
        update = write_update(
            ids, basis, [[list(sent_up)], [list(sent_down)]], [n - k, k], update, all_columns
        )
    for s in streams:
        sent_up[s], sent_down[s] = up(sent_up[s][: cols // 2]), down(sent_down[s][cols // 2 :])
    sent_up[0], update = lax.optimization_barrier((sent_up[0], update))
    update = write_update(ids, basis, [[sent_up, sent_down]], [half], update, all_columns)
    return (update, first_new, second_new)


def solution(mesh):
    n, m = mesh.shape["dp"], mesh.shape["mp"]
    ring = 4 <= n <= LONGEST_RING and n % 2 == 0 and m % 2 == 0
    placed = (
        P(("dp", "mp"), None),
        P("dp", "mp"),
        P("dp", None),
        P(("mp", "dp"), None),
        P(("mp", "dp"), None),
    )
    return jax.shard_map(
        functools.partial(on_ring, n, m) if ring else with_collectives,
        mesh=mesh,
        in_specs=placed,
        out_specs=(P("dp", "mp"), P(("mp", "dp"), None), P(("mp", "dp"), None)),
        check_vma=False,
    )
```

```python
import functools

import jax
import jax.numpy as jnp
from jax import lax
from jax.experimental import pallas as pl
from jax.experimental.pallas import tpu as pltpu
from jax.sharding import PartitionSpec as P

STEP = 1000


beta_first = 0.9
beta_second = 0.999
adam_eps = 1e-08

STREAMS = 2
LONGEST_RING = 16
SCRATCH_BYTES = 12 << 20


def adam(projected, first_moment, second_moment):
    first_new = beta_first * first_moment + (1.0 - beta_first) * projected
    second_new = beta_second * second_moment + (1.0 - beta_second) * projected * projected
    corr_first = 1.0 - beta_first**STEP
    corr_second = 1.0 - beta_second**STEP
    direction = (first_new / corr_first / (jnp.sqrt(second_new / corr_second) + adam_eps)).astype(
        jnp.bfloat16
    )
    return first_new, second_new, direction


def with_collectives(activations, grad_out, basis, first_moment, second_moment):
    own_coords = jnp.dot(
        activations, lax.all_gather(basis, "dp", axis=0, tiled=True), preferred_element_type=jnp.float32
    ).astype(jnp.bfloat16)
    coords = lax.all_gather(own_coords, "mp", axis=0, tiled=True)
    projected = lax.psum_scatter(
        lax.dot_general(
            grad_out, coords, (((0,), (0,)), ((), ())), preferred_element_type=jnp.float32
        ),
        "dp",
        scatter_dimension=0,
        tiled=True,
    )
    first_new, second_new, direction = adam(projected, first_moment, second_moment)
    update = lax.dot_general(
        basis,
        lax.all_gather(direction, "dp", axis=0, tiled=True),
        (((1,), (1,)), ((), ())),
        preferred_element_type=jnp.float32,
    ).astype(jnp.bfloat16)
    return (update, first_new, second_new)


def on_chip():
    return pl.BlockSpec(memory_space=pltpu.VMEM)


def scalars():
    return pl.BlockSpec(memory_space=pltpu.SMEM)


def ring_order(n):
    return [*range(0, n, 2), *range(n - 1, 0, -2)]


def chunk_at(here, away, n):
    index = here[0]
    step = lax.shift_right_logical(index, 1)
    place = lax.select(lax.bitwise_and(index, 1) == 0, step, n - 1 - step)
    there = lax.rem(place + away, n)
    return lax.select(there < n // 2, 2 * there, 2 * (n - 1 - there) + 1)


def kept_on_chip(arrays):
    return [pltpu.with_memory_space_constraint(a, pltpu.VMEM) for a in arrays]


def split_columns(me, activations, n):
    tokens, features = activations.shape
    part = features // n // 2

    def kernel(me_ref, own, other, kept, sent):
        kept[...] = own[...]
        sent[...] = other[...]

    half = pltpu.VMEM((tokens, features // 2), activations.dtype)
    return pl.pallas_call(
        kernel,
        out_shape=(half, half),
        grid_spec=pltpu.PrefetchScalarGridSpec(
            num_scalar_prefetch=1,
            grid=(n,),
            in_specs=[
                pl.BlockSpec((tokens, part), lambda j, me: (0, 2 * j + lax.bitwise_and(me[0], 1))),
                pl.BlockSpec((tokens, part), lambda j, me: (0, 2 * j + 1 - lax.bitwise_and(me[0], 1))),
            ],
            out_specs=(pl.BlockSpec((tokens, part), lambda j, me: (0, j)),) * 2,
        ),
        compiler_params=pltpu.CompilerParams(vmem_limit_bytes=SCRATCH_BYTES),
        name="split_columns",
    )(me, activations, activations)


def add_coords(here, me, kept, came, total, pieces, depth, n):
    tokens, width = kept.shape[0], pieces[0][0].shape[1]
    held = () if total is None else (total,)
    arrays = [piece for piece, _, _ in pieces]

    def kernel(here_ref, me_ref, *refs):
        out = refs[-1]
        side = lax.bitwise_and(me_ref[0], 1)
        refs_of = refs[2 + len(held) : -1]
        for act, place in ((refs[0], side), (refs[1], 1 - side)):
            rows = pl.ds(pl.multiple_of(place * tokens, tokens), tokens)
            acc = refs[2][rows] if held else jnp.zeros((tokens, width), jnp.float32)
            for ref, (_, away, low) in zip(refs_of, pieces, strict=True):
                start = pl.multiple_of(chunk_at(here_ref, away, n) * depth + low, 128)
                acc += jnp.dot(
                    act[:, pl.ds(start, ref.shape[0])], ref[...], preferred_element_type=jnp.float32
                )
            out[rows] = acc

    return pl.pallas_call(
        kernel,
        out_shape=pltpu.VMEM((2 * tokens, width), jnp.float32),
        in_specs=[scalars(), scalars(), *[on_chip()] * (2 + len(held) + len(arrays))],
        out_specs=on_chip(),
        cost_estimate=pl.CostEstimate(
            flops=4 * tokens * width * sum(a.shape[0] for a in arrays), transcendentals=0, bytes_accessed=4 << 20
        ),
        compiler_params=pltpu.CompilerParams(vmem_limit_bytes=SCRATCH_BYTES),
        name="add_coords",
    )(here, me, *kept_on_chip([kept, came, *held, *arrays]))


def contract_tokens(grad, coords):
    return lax.dot_general(grad, coords, (((0,), (0,)), ((), ())), preferred_element_type=jnp.float32)


def first_partials(here, me, grad_out, parts, n):
    group, width = parts[0].shape
    tokens, all_columns = grad_out.shape
    cols = all_columns // n
    groups = tokens // group

    def kernel(here_ref, me_ref, grad, *refs):
        coords, top, bottom = refs[len(parts) :]
        for k, ref in enumerate(refs[: len(parts)]):
            at = lax.rem(lax.shift_right_logical(me_ref[0], 1) + groups - k, groups)
            coords[pl.ds(pl.multiple_of(at * group, group), group)] = ref[...]
        column = pl.multiple_of(chunk_at(here_ref, n // 2, n) * cols, 128)
        part = contract_tokens(grad[:, pl.ds(column, cols)], coords[...]).astype(jnp.bfloat16)
        top[...] = part[: cols // 2]
        bottom[...] = part[cols // 2 :]

    half = pltpu.VMEM((cols // 2, width), jnp.bfloat16)
    return pl.pallas_call(
        kernel,
        out_shape=(pltpu.VMEM((tokens, width), jnp.bfloat16), half, half),
        in_specs=[scalars(), scalars(), *[on_chip()] * (1 + len(parts))],
        out_specs=(on_chip(),) * 3,
        cost_estimate=pl.CostEstimate(
            flops=2 * tokens * cols * width, transcendentals=0, bytes_accessed=4 << 20
        ),
        compiler_params=pltpu.CompilerParams(vmem_limit_bytes=SCRATCH_BYTES),
        name="first_partials",
    )(here, me, *kept_on_chip([grad_out, *parts]))


def next_partials(here, grad_out, coords, came_up, came_down, n, away):
    tokens, width = coords.shape
    cols = grad_out.shape[1] // n
    rows = came_up.shape[0]

    def kernel(here_ref, grad, coord, in_up, in_down, up, down):
        column = pl.multiple_of(chunk_at(here_ref, away, n) * cols, 128)
        part = contract_tokens(grad[:, pl.ds(column, cols)], coord[...])
        up[:rows] = (part[:rows] + in_up[...].astype(jnp.float32)).astype(jnp.bfloat16)
        if rows < cols:
            up[rows:] = part[rows:].astype(jnp.bfloat16)
        column = pl.multiple_of(chunk_at(here_ref, n - away, n) * cols, 128)
        part = contract_tokens(grad[:, pl.ds(column, cols)], coord[...])
        rest = cols - rows
        down[rest:] = (part[rest:] + in_down[...].astype(jnp.float32)).astype(jnp.bfloat16)
        if rest:
            down[:rest] = part[:rest].astype(jnp.bfloat16)

    full = pltpu.VMEM((cols, width), jnp.bfloat16)
    return pl.pallas_call(
        kernel,
        out_shape=(full, full),
        in_specs=[scalars(), *[on_chip()] * 4],
        out_specs=(on_chip(),) * 2,
        cost_estimate=pl.CostEstimate(
            flops=4 * tokens * cols * width, transcendentals=0, bytes_accessed=4 << 20
        ),
        compiler_params=pltpu.CompilerParams(vmem_limit_bytes=SCRATCH_BYTES),
        name="next_partials",
    )(here, *kept_on_chip([grad_out, coords, came_up, came_down]))


def own_direction(here, grad_out, coords, came_up, came_down, first_moment, second_moment, s, n):
    tokens, width = coords.shape
    cols = grad_out.shape[1] // n

    def kernel(here_ref, grad, coord, in_up, in_down, first, second, projected, direction):
        column = pl.multiple_of(here_ref[0] * cols, 128)
        total = (
            contract_tokens(grad[:, pl.ds(column, cols)], coord[...])
            + in_up[...].astype(jnp.float32)
            + in_down[...].astype(jnp.float32)
        )
        projected[...] = total
        mine = slice(s * width, (s + 1) * width)
        direction[...] = adam(total, first[:, mine], second[:, mine])[2]

    return pl.pallas_call(
        kernel,
        out_shape=(
            pltpu.VMEM((cols, width), jnp.float32),
            pltpu.VMEM((cols, width), jnp.bfloat16),
        ),
        in_specs=[scalars(), *[on_chip()] * 6],
        out_specs=(on_chip(),) * 2,
        cost_estimate=pl.CostEstimate(
            flops=2 * tokens * cols * width, transcendentals=0, bytes_accessed=4 << 20
        ),
        compiler_params=pltpu.CompilerParams(vmem_limit_bytes=SCRATCH_BYTES),
        name="own_direction",
    )(here, *kept_on_chip([grad_out, coords, came_up, came_down, first_moment, second_moment]))


def new_moments(projected, first_moment, second_moment):
    width = projected[0].shape[1]
    rows = first_moment.shape[0]
    tile = rows // 2
    block = pl.BlockSpec((tile, first_moment.shape[1]), lambda r: (r, 0))

    def kernel(*refs):
        first, second, first_new, second_new = refs[len(projected) :]
        for s, ref in enumerate(refs[: len(projected)]):
            mine = slice(s * width, (s + 1) * width)
            at = pl.ds(pl.multiple_of(pl.program_id(0) * tile, tile), tile)
            first_new[:, mine], second_new[:, mine], _ = adam(ref[at], first[at, mine], second[at, mine])

    return pl.pallas_call(
        kernel,
        out_shape=(jax.ShapeDtypeStruct(first_moment.shape, jnp.float32),) * 2,
        grid=(rows // tile,),
        in_specs=[on_chip()] * (len(projected) + 2),
        out_specs=(block, block),
        cost_estimate=pl.CostEstimate(flops=0, transcendentals=0, bytes_accessed=6 << 20),
        compiler_params=pltpu.CompilerParams(vmem_limit_bytes=SCRATCH_BYTES),
        name="new_moments",
    )(*kept_on_chip([*projected, first_moment, second_moment]))


def write_update(here, basis, chunks, places, update, all_columns):
    depth, rank = basis.shape
    cols = sum(row[0].shape[0] for row in chunks[0])
    flat = [stream for chunk in chunks for row in chunk for stream in row]
    held = () if update is None else (update,)
    tile = depth // 2

    def kernel(here_ref, base, *refs):
        out = refs[-1]
        left = list(refs[: len(flat)])
        lines = pl.ds(pl.multiple_of(pl.program_id(1) * tile, tile), tile)
        for g, chunk in enumerate(chunks):
            rows = [[left.pop(0) for _ in row] for row in chunk]

            @pl.when(pl.program_id(0) == g)
            def _(rows=rows):
                whole = jnp.concatenate(
                    [jnp.concatenate([stream[...] for stream in row], axis=1) for row in rows], axis=0
                )
                out[...] = lax.dot_general(
                    base[lines], whole, (((1,), (1,)), ((), ())), preferred_element_type=jnp.float32
                ).astype(out.dtype)

    n = all_columns // cols

    def place(g, r, here):
        at = chunk_at(here, places[0], n)
        for k in range(1, len(places)):
            at = jnp.where(g == k, chunk_at(here, places[k], n), at)
        return (r, at)

    return pl.pallas_call(
        kernel,
        out_shape=jax.ShapeDtypeStruct((depth, all_columns), jnp.bfloat16),
        grid_spec=pltpu.PrefetchScalarGridSpec(
            num_scalar_prefetch=1,
            grid=(len(chunks), depth // tile),
            in_specs=[
                *[on_chip()] * (1 + len(flat)),
                *[pl.BlockSpec(memory_space=pl.ANY)] * len(held),
            ],
            out_specs=pl.BlockSpec((tile, cols), place),
        ),
        input_output_aliases={2 + len(flat): 0} if held else {},
        cost_estimate=pl.CostEstimate(
            flops=2 * depth * cols * rank * len(chunks),
            transcendentals=0,
            bytes_accessed=2 * depth * cols * len(chunks),
        ),
        compiler_params=pltpu.CompilerParams(vmem_limit_bytes=SCRATCH_BYTES),
        name="write_update",
    )(here, *kept_on_chip([basis, *flat]), *held)


def on_ring(n, m, activations, grad_out, basis, first_moment, second_moment):
    order = ring_order(n)
    upward = [(order[k], order[(k + 1) % n]) for k in range(n)]
    downward = [(b, a) for a, b in upward]
    partners = [(k, k ^ 1) for k in range(m)]

    def hop(to_up, to_down):
        return (lax.ppermute(to_up, "dp", upward), lax.ppermute(to_down, "dp", downward))

    me = lax.axis_index("mp")
    here, me, side, activations, basis = lax.optimization_barrier(
        (lax.axis_index("dp").reshape(1), me.reshape(1), lax.bitwise_and(me, 1), activations, basis)
    )

    depth, rank = basis.shape
    width = rank // STREAMS
    all_columns = grad_out.shape[1]
    cols = all_columns // n
    half = n // 2
    streams = range(STREAMS)

    part = depth // 2
    own = lax.dynamic_slice(basis, (side * part, 0), (part, rank))
    own = [own[:, s * width : (s + 1) * width] for s in streams]
    ups, downs = list(own), list(own)
    pieces = [[(own[s], 0, 0)] for s in streams]
    kept, sent = split_columns(me, activations, n)
    came = lax.ppermute(sent, "mp", partners)
    total = [None] * STREAMS
    for k in range(1, half + 1):
        for s in streams:
            low = 0
            if k == half:
                low = part // 2
                ups[s], downs[s] = ups[s][:low], downs[s][low:]
                total[s] = add_coords(here, me, kept, came, None, pieces[s], part, n)
                pieces[s] = []
            ups[s], downs[s] = hop(ups[s], downs[s])
            pieces[s] += [(ups[s], n - k, 0), (downs[s], k, low)]
    for s in streams:
        total[s] = add_coords(here, me, kept, came, total[s], pieces[s], part, n)

    parts = [None] * STREAMS
    for s in streams:
        other = lax.ppermute(total[s], "mp", partners)
        pair = (total[s] + other).astype(jnp.bfloat16)
        parts[s] = [pair] + [lax.ppermute(pair, "mp", [(a, (a + k) % m) for a in range(m)]) for k in range(2, m, 2)]

    coords = [None] * STREAMS
    for s in streams:
        coords[s], ups[s], downs[s] = first_partials(here, me, grad_out, parts[s], n)
        ups[s], downs[s] = hop(ups[s], downs[s])
    for k in range(2, half + 1):
        for s in streams:
            ups[s], downs[s] = next_partials(here, grad_out, coords[s], ups[s], downs[s], n, half + 1 - k)
            ups[s], downs[s] = hop(ups[s], downs[s])
    projected = [None] * STREAMS
    direction = [None] * STREAMS
    for s in streams:
        projected[s], direction[s] = own_direction(
            here, grad_out, coords[s], ups[s], downs[s], first_moment, second_moment, s, n,
        )

    ups, downs = list(direction), list(direction)
    update = write_update(here, basis, [[direction]], [0], None, all_columns)
    first_new, second_new = new_moments(projected, first_moment, second_moment)
    for k in range(1, half):
        for s in streams:
            ups[s], downs[s] = hop(ups[s], downs[s])
        update = write_update(here, basis, [[list(ups)], [list(downs)]], [n - k, k], update, all_columns)
    for s in streams:
        ups[s], downs[s] = hop(ups[s][: cols // 2], downs[s][cols // 2 :])
    update = write_update(here, basis, [[ups, downs]], [half], update, all_columns)
    return (update, first_new, second_new)


def solution(mesh):
    n, m = mesh.shape["dp"], mesh.shape["mp"]
    ring = 4 <= n <= LONGEST_RING and n % 2 == 0 and m % 2 == 0
    placed = (
        P(("dp", "mp"), None),
        P("dp", "mp"),
        P("dp", None),
        P(("mp", "dp"), None),
        P(("mp", "dp"), None),
    )
    return jax.shard_map(
        functools.partial(on_ring, n, m) if ring else with_collectives,
        mesh=mesh,
        in_specs=placed,
        out_specs=(P("dp", "mp"), P(("mp", "dp"), None), P(("mp", "dp"), None)),
        check_vma=False,
    )
```

```python
import functools

import jax
import jax.numpy as jnp
from jax import lax
from jax.experimental import pallas as pl
from jax.experimental.pallas import tpu as pltpu
from jax.sharding import PartitionSpec as P

STEP = 1000


beta_first = 0.9
beta_second = 0.999
adam_eps = 1e-08

STREAMS = 2
LONGEST_RING = 16
SCRATCH_BYTES = 12 << 20


def adam(projected, first_moment, second_moment):
    first_new = beta_first * first_moment + (1.0 - beta_first) * projected
    second_new = beta_second * second_moment + (1.0 - beta_second) * projected * projected
    corr_first = 1.0 - beta_first**STEP
    corr_second = 1.0 - beta_second**STEP
    direction = (first_new / corr_first / (jnp.sqrt(second_new / corr_second) + adam_eps)).astype(
        jnp.bfloat16
    )
    return first_new, second_new, direction


def with_collectives(activations, grad_out, basis, first_moment, second_moment):
    own_coords = jnp.dot(
        activations, lax.all_gather(basis, "dp", axis=0, tiled=True), preferred_element_type=jnp.float32
    ).astype(jnp.bfloat16)
    coords = lax.all_gather(own_coords, "mp", axis=0, tiled=True)
    projected = lax.psum_scatter(
        lax.dot_general(
            grad_out, coords, (((0,), (0,)), ((), ())), preferred_element_type=jnp.float32
        ),
        "dp",
        scatter_dimension=0,
        tiled=True,
    )
    first_new, second_new, direction = adam(projected, first_moment, second_moment)
    update = lax.dot_general(
        basis,
        lax.all_gather(direction, "dp", axis=0, tiled=True),
        (((1,), (1,)), ((), ())),
        preferred_element_type=jnp.float32,
    ).astype(jnp.bfloat16)
    return (update, first_new, second_new)


def on_chip():
    return pl.BlockSpec(memory_space=pltpu.VMEM)


def scalars():
    return pl.BlockSpec(memory_space=pltpu.SMEM)


def left_in_hbm(array):
    return pltpu.with_memory_space_constraint(array, pltpu.HBM)


def ring_order(n):
    return [*range(0, n, 2), *range(n - 1, 0, -2)]


def chunk_at(here, away, n):
    index = here[0]
    step = lax.shift_right_logical(index, 1)
    place = lax.select(lax.bitwise_and(index, 1) == 0, step, n - 1 - step)
    there = lax.rem(place + away, n)
    return lax.select(there < n // 2, 2 * there, 2 * (n - 1 - there) + 1)


def kept_on_chip(arrays):
    return [pltpu.with_memory_space_constraint(a, pltpu.VMEM) for a in arrays]


def split_columns(me, activations, n):
    tokens, features = activations.shape
    part = features // n // 2
    half = pltpu.VMEM((tokens, features // 2), activations.dtype)

    def kernel(me_ref, source, kept, sent, sems):
        side = lax.bitwise_and(me_ref[0], 1)
        copies = []
        for way, (out, which) in enumerate(((sent, 1 - side), (kept, side))):
            for j in range(n):
                columns = pl.ds(pl.multiple_of((2 * j + which) * part, 128), part)
                copies.append(
                    pltpu.make_async_copy(
                        source.at[:, columns], out.at[:, pl.ds(j * part, part)], sems.at[way, j]
                    )
                )
        for copy in copies:
            copy.start()
        for copy in copies:
            copy.wait()

    return pl.pallas_call(
        kernel,
        out_shape=(half, half),
        in_specs=[scalars(), pl.BlockSpec(memory_space=pltpu.HBM)],
        out_specs=(on_chip(),) * 2,
        scratch_shapes=[pltpu.SemaphoreType.DMA((2, n))],
        compiler_params=pltpu.CompilerParams(vmem_limit_bytes=SCRATCH_BYTES),
        name="split_columns",
    )(me, left_in_hbm(activations))


def own_pieces(me, basis):
    depth, rank = basis.shape
    piece = pltpu.VMEM((depth // 2, rank // STREAMS), basis.dtype)

    def kernel(me_ref, source, *refs):
        rows = pl.ds(pl.multiple_of(lax.bitwise_and(me_ref[0], 1) * (depth // 2), depth // 2), depth // 2)
        width = rank // STREAMS
        copies = [
            pltpu.make_async_copy(source.at[rows, pl.ds(s * width, width)], refs[s], refs[-1].at[s])
            for s in range(STREAMS)
        ]
        for copy in copies:
            copy.start()
        for copy in copies:
            copy.wait()

    return pl.pallas_call(
        kernel,
        out_shape=(piece,) * STREAMS,
        in_specs=[scalars(), pl.BlockSpec(memory_space=pltpu.HBM)],
        out_specs=(on_chip(),) * STREAMS,
        scratch_shapes=[pltpu.SemaphoreType.DMA((STREAMS,))],
        compiler_params=pltpu.CompilerParams(vmem_limit_bytes=SCRATCH_BYTES),
        name="own_pieces",
    )(me, left_in_hbm(basis))


def add_coords(here, me, kept, came, total, pieces, depth, n):
    tokens, width = kept.shape[0], pieces[0][0].shape[1]
    held = () if total is None else (total,)
    arrays = [piece for piece, _, _ in pieces]

    def kernel(here_ref, me_ref, *refs):
        out = refs[-1]
        side = lax.bitwise_and(me_ref[0], 1)
        refs_of = refs[2 + len(held) : -1]
        for act, place in ((refs[0], side), (refs[1], 1 - side)):
            rows = pl.ds(pl.multiple_of(place * tokens, tokens), tokens)
            acc = refs[2][rows] if held else jnp.zeros((tokens, width), jnp.float32)
            for ref, (_, away, low) in zip(refs_of, pieces, strict=True):
                start = pl.multiple_of(chunk_at(here_ref, away, n) * depth + low, 128)
                acc += jnp.dot(
                    act[:, pl.ds(start, ref.shape[0])], ref[...], preferred_element_type=jnp.float32
                )
            out[rows] = acc

    return pl.pallas_call(
        kernel,
        out_shape=pltpu.VMEM((2 * tokens, width), jnp.float32),
        in_specs=[scalars(), scalars(), *[on_chip()] * (2 + len(held) + len(arrays))],
        out_specs=on_chip(),
        cost_estimate=pl.CostEstimate(
            flops=4 * tokens * width * sum(a.shape[0] for a in arrays), transcendentals=0, bytes_accessed=4 << 20
        ),
        compiler_params=pltpu.CompilerParams(vmem_limit_bytes=SCRATCH_BYTES),
        name="add_coords",
    )(here, me, *kept_on_chip([kept, came, *held, *arrays]))


def contract_tokens(grad, coords):
    return lax.dot_general(grad, coords, (((0,), (0,)), ((), ())), preferred_element_type=jnp.float32)


def first_partials(here, me, grad_out, parts, n):
    group, width = parts[0].shape
    tokens, all_columns = grad_out.shape
    cols = all_columns // n
    groups = tokens // group

    def kernel(here_ref, me_ref, grad, *refs):
        coords, top, bottom = refs[len(parts) :]
        for k, ref in enumerate(refs[: len(parts)]):
            at = lax.rem(lax.shift_right_logical(me_ref[0], 1) + groups - k, groups)
            coords[pl.ds(pl.multiple_of(at * group, group), group)] = ref[...]
        column = pl.multiple_of(chunk_at(here_ref, n // 2, n) * cols, 128)
        part = contract_tokens(grad[:, pl.ds(column, cols)], coords[...]).astype(jnp.bfloat16)
        top[...] = part[: cols // 2]
        bottom[...] = part[cols // 2 :]

    half = pltpu.VMEM((cols // 2, width), jnp.bfloat16)
    return pl.pallas_call(
        kernel,
        out_shape=(pltpu.VMEM((tokens, width), jnp.bfloat16), half, half),
        in_specs=[scalars(), scalars(), *[on_chip()] * (1 + len(parts))],
        out_specs=(on_chip(),) * 3,
        cost_estimate=pl.CostEstimate(
            flops=2 * tokens * cols * width, transcendentals=0, bytes_accessed=4 << 20
        ),
        compiler_params=pltpu.CompilerParams(vmem_limit_bytes=SCRATCH_BYTES),
        name="first_partials",
    )(here, me, *kept_on_chip([grad_out, *parts]))


def next_partials(here, grad_out, coords, came, n, away, upward):
    tokens, width = coords.shape
    cols = grad_out.shape[1] // n
    rows = came.shape[0]
    added = slice(0, rows) if upward else slice(cols - rows, cols)
    rest = slice(rows, cols) if upward else slice(0, cols - rows)

    def kernel(here_ref, grad, coord, arrived, out):
        column = pl.multiple_of(chunk_at(here_ref, away if upward else n - away, n) * cols, 128)
        part = contract_tokens(grad[:, pl.ds(column, cols)], coord[...])
        out[added] = (part[added] + arrived[...].astype(jnp.float32)).astype(jnp.bfloat16)
        if rows < cols:
            out[rest] = part[rest].astype(jnp.bfloat16)

    return pl.pallas_call(
        kernel,
        out_shape=pltpu.VMEM((cols, width), jnp.bfloat16),
        in_specs=[scalars(), *[on_chip()] * 3],
        out_specs=on_chip(),
        cost_estimate=pl.CostEstimate(
            flops=2 * tokens * cols * width, transcendentals=0, bytes_accessed=2 << 20
        ),
        compiler_params=pltpu.CompilerParams(vmem_limit_bytes=SCRATCH_BYTES),
        name="next_partials",
    )(here, *kept_on_chip([grad_out, coords, came]))


def own_direction(here, grad_out, coords, came_up, came_down, first_moment, second_moment, s, n):
    tokens, width = coords.shape
    cols = grad_out.shape[1] // n

    def kernel(here_ref, grad, coord, in_up, in_down, first, second, projected, direction):
        column = pl.multiple_of(here_ref[0] * cols, 128)
        total = (
            contract_tokens(grad[:, pl.ds(column, cols)], coord[...])
            + in_up[...].astype(jnp.float32)
            + in_down[...].astype(jnp.float32)
        )
        projected[...] = total
        mine = slice(s * width, (s + 1) * width)
        direction[...] = adam(total, first[:, mine], second[:, mine])[2]

    return pl.pallas_call(
        kernel,
        out_shape=(
            pltpu.VMEM((cols, width), jnp.float32),
            pltpu.VMEM((cols, width), jnp.bfloat16),
        ),
        in_specs=[scalars(), *[on_chip()] * 6],
        out_specs=(on_chip(),) * 2,
        cost_estimate=pl.CostEstimate(
            flops=2 * tokens * cols * width, transcendentals=0, bytes_accessed=4 << 20
        ),
        compiler_params=pltpu.CompilerParams(vmem_limit_bytes=SCRATCH_BYTES),
        name="own_direction",
    )(here, *kept_on_chip([grad_out, coords, came_up, came_down, first_moment, second_moment]))


def new_moments(projected, first_moment, second_moment):
    width = projected[0].shape[1]
    rows = first_moment.shape[0]
    tile = rows // 2
    block = pl.BlockSpec((tile, first_moment.shape[1]), lambda r: (r, 0))

    def kernel(*refs):
        first, second, first_new, second_new = refs[len(projected) :]
        for s, ref in enumerate(refs[: len(projected)]):
            mine = slice(s * width, (s + 1) * width)
            at = pl.ds(pl.multiple_of(pl.program_id(0) * tile, tile), tile)
            first_new[:, mine], second_new[:, mine], _ = adam(ref[at], first[at, mine], second[at, mine])

    return pl.pallas_call(
        kernel,
        out_shape=(jax.ShapeDtypeStruct(first_moment.shape, jnp.float32),) * 2,
        grid=(rows // tile,),
        in_specs=[on_chip()] * (len(projected) + 2),
        out_specs=(block, block),
        cost_estimate=pl.CostEstimate(flops=0, transcendentals=0, bytes_accessed=6 << 20),
        compiler_params=pltpu.CompilerParams(vmem_limit_bytes=SCRATCH_BYTES),
        name="new_moments",
    )(*kept_on_chip([*projected, first_moment, second_moment]))


def write_update(here, basis, chunks, places, update, all_columns):
    depth, rank = basis.shape
    cols = sum(row[0].shape[0] for row in chunks[0])
    flat = [stream for chunk in chunks for row in chunk for stream in row]
    held = () if update is None else (update,)
    n = all_columns // cols
    starts = range(0, cols, 256)
    blocks = [(low, min(256, cols - low)) for low in starts]

    def kernel(here_ref, base, *refs):
        out, made, sems = refs[-3:]
        left = list(refs[: len(flat)])
        copies = []
        for g, chunk in enumerate(chunks):
            rows = [[left.pop(0) for _ in row] for row in chunk]
            whole = jnp.concatenate(
                [jnp.concatenate([stream[...] for stream in row], axis=1) for row in rows], axis=0
            )
            column = chunk_at(here_ref, places[g], n) * cols
            for b, (low, size) in enumerate(blocks):
                made[g, :, low : low + size] = lax.dot_general(
                    base[...],
                    whole[low : low + size],
                    (((1,), (1,)), ((), ())),
                    preferred_element_type=jnp.float32,
                ).astype(made.dtype)
                columns = pl.ds(pl.multiple_of(column + low, 128), size)
                copy = pltpu.make_async_copy(
                    made.at[g, :, pl.ds(low, size)], out.at[:, columns], sems.at[g, b]
                )
                copy.start()
                copies.append(copy)
        for copy in copies:
            copy.wait()

    return pl.pallas_call(
        kernel,
        out_shape=jax.ShapeDtypeStruct((depth, all_columns), jnp.bfloat16),
        in_specs=[
            scalars(),
            *[on_chip()] * (1 + len(flat)),
            *[pl.BlockSpec(memory_space=pl.ANY)] * len(held),
        ],
        out_specs=pl.BlockSpec(memory_space=pl.ANY),
        scratch_shapes=[
            pltpu.VMEM((len(chunks), depth, cols), jnp.bfloat16),
            pltpu.SemaphoreType.DMA((len(chunks), len(blocks))),
        ],
        input_output_aliases={2 + len(flat): 0} if held else {},
        cost_estimate=pl.CostEstimate(
            flops=2 * depth * cols * rank * len(chunks),
            transcendentals=0,
            bytes_accessed=2 * depth * cols * len(chunks),
        ),
        compiler_params=pltpu.CompilerParams(vmem_limit_bytes=SCRATCH_BYTES),
        name="write_update",
    )(here, *kept_on_chip([basis, *flat]), *held)


def on_ring(n, m, activations, grad_out, basis, first_moment, second_moment):
    order = ring_order(n)
    upward = [(order[k], order[(k + 1) % n]) for k in range(n)]
    downward = [(b, a) for a, b in upward]
    partners = [(k, k ^ 1) for k in range(m)]

    def hop(to_up, to_down):
        return (lax.ppermute(to_up, "dp", upward), lax.ppermute(to_down, "dp", downward))

    me = lax.axis_index("mp")
    here, me, activations, basis = lax.optimization_barrier(
        (lax.axis_index("dp").reshape(1), me.reshape(1), activations, basis)
    )

    depth, _ = basis.shape
    all_columns = grad_out.shape[1]
    cols = all_columns // n
    half = n // 2
    streams = range(STREAMS)

    part = depth // 2
    own = own_pieces(me, basis)
    ups, downs = list(own), list(own)
    pieces = [[(own[s], 0, 0)] for s in streams]
    kept, sent = split_columns(me, activations, n)
    swapped = lax.ppermute(sent, "mp", partners)
    total = [None] * STREAMS
    for k in range(1, half + 1):
        for s in streams:
            low = 0
            if k == half:
                low = part // 2
                ups[s], downs[s] = ups[s][:low], downs[s][low:]
                total[s] = add_coords(here, me, kept, swapped, None, pieces[s], part, n)
                pieces[s] = []
            ups[s], downs[s] = hop(ups[s], downs[s])
            pieces[s] += [(ups[s], n - k, 0), (downs[s], k, low)]
    for s in streams:
        total[s] = add_coords(here, me, kept, swapped, total[s], pieces[s], part, n)

    parts = [None] * STREAMS
    for s in streams:
        other = lax.ppermute(total[s], "mp", partners)
        pair = (total[s] + other).astype(jnp.bfloat16)
        parts[s] = [pair] + [lax.ppermute(pair, "mp", [(a, (a + k) % m) for a in range(m)]) for k in range(2, m, 2)]

    coords = [None] * STREAMS
    for s in streams:
        coords[s], ups[s], downs[s] = first_partials(here, me, grad_out, parts[s], n)
        ups[s], downs[s] = hop(ups[s], downs[s])
    for k in range(2, half + 1):
        for s in streams:
            ups[s], downs[s] = [
                next_partials(here, grad_out, coords[s], came, n, half + 1 - k, way == "up")
                for way, came in (("up", ups[s]), ("down", downs[s]))
            ]
            ups[s], downs[s] = hop(ups[s], downs[s])
    projected = [None] * STREAMS
    direction = [None] * STREAMS
    for s in streams:
        projected[s], direction[s] = own_direction(
            here, grad_out, coords[s], ups[s], downs[s], first_moment, second_moment, s, n,
        )

    ups, downs = list(direction), list(direction)
    update = write_update(here, basis, [[direction]], [0], None, all_columns)
    first_new, second_new = new_moments(projected, first_moment, second_moment)
    for k in range(1, half):
        for s in streams:
            ups[s], downs[s] = hop(ups[s], downs[s])
        update = write_update(here, basis, [[list(ups)], [list(downs)]], [n - k, k], update, all_columns)
    for s in streams:
        ups[s], downs[s] = hop(ups[s][: cols // 2], downs[s][cols // 2 :])
    update = write_update(here, basis, [[ups, downs]], [half], update, all_columns)
    return (update, first_new, second_new)


def solution(mesh):
    n, m = mesh.shape["dp"], mesh.shape["mp"]
    ring = 4 <= n <= LONGEST_RING and n % 2 == 0 and m % 2 == 0
    placed = (
        P(("dp", "mp"), None),
        P("dp", "mp"),
        P("dp", None),
        P(("mp", "dp"), None),
        P(("mp", "dp"), None),
    )
    return jax.shard_map(
        functools.partial(on_ring, n, m) if ring else with_collectives,
        mesh=mesh,
        in_specs=placed,
        out_specs=(P("dp", "mp"), P(("mp", "dp"), None), P(("mp", "dp"), None)),
        check_vma=False,
    )
```

```python
import functools

import jax
import jax.numpy as jnp
from jax import lax
from jax.experimental import pallas as pl
from jax.experimental.pallas import tpu as pltpu
from jax.sharding import PartitionSpec as P

STEP = 1000


beta_first = 0.9
beta_second = 0.999
adam_eps = 1e-08

STREAMS = 2
LONGEST_RING = 16
SCRATCH_BYTES = 12 << 20


def adam(projected, first_moment, second_moment):
    first_new = beta_first * first_moment + (1.0 - beta_first) * projected
    second_new = beta_second * second_moment + (1.0 - beta_second) * projected * projected
    corr_first = 1.0 - beta_first**STEP
    corr_second = 1.0 - beta_second**STEP
    direction = (first_new / corr_first / (jnp.sqrt(second_new / corr_second) + adam_eps)).astype(
        jnp.bfloat16
    )
    return first_new, second_new, direction


def with_collectives(activations, grad_out, basis, first_moment, second_moment):
    own_coords = jnp.dot(
        activations, lax.all_gather(basis, "dp", axis=0, tiled=True), preferred_element_type=jnp.float32
    ).astype(jnp.bfloat16)
    coords = lax.all_gather(own_coords, "mp", axis=0, tiled=True)
    projected = lax.psum_scatter(
        lax.dot_general(
            grad_out, coords, (((0,), (0,)), ((), ())), preferred_element_type=jnp.float32
        ),
        "dp",
        scatter_dimension=0,
        tiled=True,
    )
    first_new, second_new, direction = adam(projected, first_moment, second_moment)
    update = lax.dot_general(
        basis,
        lax.all_gather(direction, "dp", axis=0, tiled=True),
        (((1,), (1,)), ((), ())),
        preferred_element_type=jnp.float32,
    ).astype(jnp.bfloat16)
    return (update, first_new, second_new)


def on_chip():
    return pl.BlockSpec(memory_space=pltpu.VMEM)


def scalars():
    return pl.BlockSpec(memory_space=pltpu.SMEM)


def left_in_hbm(array):
    return pltpu.with_memory_space_constraint(array, pltpu.HBM)


def ring_order(n):
    return [*range(0, n, 2), *range(n - 1, 0, -2)]


def chunk_at(here, away, n):
    index = here[0]
    step = lax.shift_right_logical(index, 1)
    place = lax.select(lax.bitwise_and(index, 1) == 0, step, n - 1 - step)
    there = lax.rem(place + away, n)
    return lax.select(there < n // 2, 2 * there, 2 * (n - 1 - there) + 1)


def kept_on_chip(arrays):
    return [pltpu.with_memory_space_constraint(a, pltpu.VMEM) for a in arrays]


def split_columns(here, me, activations, n):
    tokens, features = activations.shape
    depth = features // n
    part = depth // 2
    near = pltpu.VMEM((tokens, part + (n // 2 - 1) * depth), activations.dtype)
    far = pltpu.VMEM((tokens, depth), activations.dtype)

    def kernel(here_ref, me_ref, source, kept, sent, farthest, sems):
        mine = lax.bitwise_and(me_ref[0], 1)
        copies = []

        def copy(start, size, out, low):
            columns = pl.ds(pl.multiple_of(start, 128), size)
            copies.append(
                pltpu.make_async_copy(source.at[:, columns], out.at[:, pl.ds(low, size)], sems.at[len(copies)])
            )

        copy(chunk_at(here_ref, n // 2, n) * depth, depth, farthest, 0)
        for out, side in ((sent, 1 - mine), (kept, mine)):
            copy(here_ref[0] * depth + side * part, part, out, 0)
            for k in range(1, n // 2):
                block = chunk_at(here_ref, lax.select(side == 0, n - k, k), n)
                copy(block * depth, depth, out, part + (k - 1) * depth)
        for one in copies:
            one.start()
        for one in copies:
            one.wait()

    return pl.pallas_call(
        kernel,
        out_shape=(near, near, far),
        in_specs=[scalars(), scalars(), pl.BlockSpec(memory_space=pltpu.HBM)],
        out_specs=(on_chip(),) * 3,
        scratch_shapes=[pltpu.SemaphoreType.DMA((n + 1,))],
        compiler_params=pltpu.CompilerParams(vmem_limit_bytes=SCRATCH_BYTES),
        name="split_columns",
    )(here, me, left_in_hbm(activations))


def own_pieces(basis):
    depth, rank = basis.shape
    width = rank // STREAMS

    def kernel(source, *refs):
        copies = [
            pltpu.make_async_copy(source.at[:, pl.ds(s * width, width)], refs[s], refs[-1].at[s])
            for s in range(STREAMS)
        ]
        for copy in copies:
            copy.start()
        for copy in copies:
            copy.wait()

    return pl.pallas_call(
        kernel,
        out_shape=(pltpu.VMEM((depth, width), basis.dtype),) * STREAMS,
        in_specs=[pl.BlockSpec(memory_space=pltpu.HBM)],
        out_specs=(on_chip(),) * STREAMS,
        scratch_shapes=[pltpu.SemaphoreType.DMA((STREAMS,))],
        compiler_params=pltpu.CompilerParams(vmem_limit_bytes=SCRATCH_BYTES),
        name="own_pieces",
    )(left_in_hbm(basis))


def half_rows(me, block):
    part = block.shape[0] // 2

    def kernel(me_ref, source, out):
        out[...] = source[pl.ds(pl.multiple_of(lax.bitwise_and(me_ref[0], 1) * part, part), part)]

    return pl.pallas_call(
        kernel,
        out_shape=pltpu.VMEM((part, block.shape[1]), block.dtype),
        in_specs=[scalars(), on_chip()],
        out_specs=on_chip(),
        compiler_params=pltpu.CompilerParams(vmem_limit_bytes=SCRATCH_BYTES),
        name="half_rows",
    )(me, *kept_on_chip([block]))


def add_coords(me, kept, came, total, pieces):
    tokens, width = kept.shape[0], pieces[0][0].shape[1]
    held = () if total is None else (total,)
    arrays = [piece for piece, _, _ in pieces]

    def kernel(me_ref, *refs):
        out = refs[-1]
        side = lax.bitwise_and(me_ref[0], 1)
        refs_of = refs[2 + len(held) : -1]
        for act, place in ((refs[0], side), (refs[1], 1 - side)):
            rows = pl.ds(pl.multiple_of(place * tokens, tokens), tokens)
            acc = refs[2][rows] if held else jnp.zeros((tokens, width), jnp.float32)
            for ref, (_, low, size) in zip(refs_of, pieces, strict=True):
                own = pl.ds(pl.multiple_of(side * size, size), size) if size < ref.shape[0] else slice(None)
                acc += jnp.dot(act[:, low : low + size], ref[own], preferred_element_type=jnp.float32)
            out[rows] = acc

    return pl.pallas_call(
        kernel,
        out_shape=pltpu.VMEM((2 * tokens, width), jnp.float32),
        in_specs=[scalars(), *[on_chip()] * (2 + len(held) + len(arrays))],
        out_specs=on_chip(),
        cost_estimate=pl.CostEstimate(
            flops=4 * tokens * width * sum(size for _, _, size in pieces), transcendentals=0, bytes_accessed=4 << 20
        ),
        compiler_params=pltpu.CompilerParams(vmem_limit_bytes=SCRATCH_BYTES),
        name="add_coords",
    )(me, *kept_on_chip([kept, came, *held, *arrays]))


def contract_tokens(grad, coords):
    return lax.dot_general(grad, coords, (((0,), (0,)), ((), ())), preferred_element_type=jnp.float32)


def first_partials(here, me, grad_out, sums, fars, lasts, n, m):
    group, width = sums[0].shape
    tokens, all_columns = grad_out.shape
    own_tokens = group // 2
    cols = all_columns // n
    part = lasts[0].shape[0]

    def kernel(here_ref, me_ref, grad, *refs):
        coords, top, bottom = refs[-3:]
        own_last, other_last = refs[-5:-3]
        side = lax.bitwise_and(me_ref[0], 1)
        own_columns = pl.ds(pl.multiple_of(side * part, part), part)
        other_columns = pl.ds(pl.multiple_of((1 - side) * part, part), part)
        for k, pair in enumerate(refs[: len(sums)]):
            first = lax.rem(lax.bitwise_and(me_ref[0], ~1) + m - 2 * k, m)
            for place, far in zip((side, 1 - side), refs[len(sums) + 2 * k :][:2], strict=True):
                total = (
                    pair[pl.ds(pl.multiple_of(place * own_tokens, own_tokens), own_tokens)]
                    + jnp.dot(far[:, own_columns], own_last[...], preferred_element_type=jnp.float32)
                    + jnp.dot(far[:, other_columns], other_last[...], preferred_element_type=jnp.float32)
                )
                low = pl.multiple_of((first + place) * own_tokens, own_tokens)
                coords[pl.ds(low, own_tokens)] = total.astype(jnp.bfloat16)
        column = pl.multiple_of(chunk_at(here_ref, n // 2, n) * cols, 128)
        sent = contract_tokens(grad[:, pl.ds(column, cols)], coords[...]).astype(jnp.bfloat16)
        top[...] = sent[: cols // 2]
        bottom[...] = sent[cols // 2 :]

    half = pltpu.VMEM((cols // 2, width), jnp.bfloat16)
    arrays = [grad_out, *sums, *fars, *lasts]
    return pl.pallas_call(
        kernel,
        out_shape=(pltpu.VMEM((tokens, width), jnp.bfloat16), half, half),
        in_specs=[scalars(), scalars(), *[on_chip()] * len(arrays)],
        out_specs=(on_chip(),) * 3,
        cost_estimate=pl.CostEstimate(
            flops=2 * tokens * (cols + 2 * part) * width, transcendentals=0, bytes_accessed=4 << 20
        ),
        compiler_params=pltpu.CompilerParams(vmem_limit_bytes=SCRATCH_BYTES),
        name="first_partials",
    )(here, me, *kept_on_chip(arrays))


def next_partials(here, grad_out, coords, came, n, away, upward):
    tokens, width = coords.shape
    cols = grad_out.shape[1] // n
    rows = came.shape[0]
    added = slice(0, rows) if upward else slice(cols - rows, cols)
    rest = slice(rows, cols) if upward else slice(0, cols - rows)

    def kernel(here_ref, grad, coord, arrived, out):
        column = pl.multiple_of(chunk_at(here_ref, away if upward else n - away, n) * cols, 128)
        part = contract_tokens(grad[:, pl.ds(column, cols)], coord[...])
        out[added] = (part[added] + arrived[...].astype(jnp.float32)).astype(jnp.bfloat16)
        if rows < cols:
            out[rest] = part[rest].astype(jnp.bfloat16)

    return pl.pallas_call(
        kernel,
        out_shape=pltpu.VMEM((cols, width), jnp.bfloat16),
        in_specs=[scalars(), *[on_chip()] * 3],
        out_specs=on_chip(),
        cost_estimate=pl.CostEstimate(
            flops=2 * tokens * cols * width, transcendentals=0, bytes_accessed=2 << 20
        ),
        compiler_params=pltpu.CompilerParams(vmem_limit_bytes=SCRATCH_BYTES),
        name="next_partials",
    )(here, *kept_on_chip([grad_out, coords, came]))


def own_direction(here, grad_out, coords, came_up, came_down, first_moment, second_moment, s, n):
    tokens, width = coords.shape
    cols = grad_out.shape[1] // n

    def kernel(here_ref, grad, coord, in_up, in_down, first, second, projected, direction):
        column = pl.multiple_of(here_ref[0] * cols, 128)
        total = (
            contract_tokens(grad[:, pl.ds(column, cols)], coord[...])
            + in_up[...].astype(jnp.float32)
            + in_down[...].astype(jnp.float32)
        )
        projected[...] = total
        mine = slice(s * width, (s + 1) * width)
        direction[...] = adam(total, first[:, mine], second[:, mine])[2]

    return pl.pallas_call(
        kernel,
        out_shape=(
            pltpu.VMEM((cols, width), jnp.float32),
            pltpu.VMEM((cols, width), jnp.bfloat16),
        ),
        in_specs=[scalars(), *[on_chip()] * 6],
        out_specs=(on_chip(),) * 2,
        cost_estimate=pl.CostEstimate(
            flops=2 * tokens * cols * width, transcendentals=0, bytes_accessed=4 << 20
        ),
        compiler_params=pltpu.CompilerParams(vmem_limit_bytes=SCRATCH_BYTES),
        name="own_direction",
    )(here, *kept_on_chip([grad_out, coords, came_up, came_down, first_moment, second_moment]))


def new_moments(projected, first_moment, second_moment):
    width = projected[0].shape[1]
    rows = first_moment.shape[0]
    tile = rows // 2
    block = pl.BlockSpec((tile, first_moment.shape[1]), lambda r: (r, 0))

    def kernel(*refs):
        first, second, first_new, second_new = refs[len(projected) :]
        for s, ref in enumerate(refs[: len(projected)]):
            mine = slice(s * width, (s + 1) * width)
            at = pl.ds(pl.multiple_of(pl.program_id(0) * tile, tile), tile)
            first_new[:, mine], second_new[:, mine], _ = adam(ref[at], first[at, mine], second[at, mine])

    return pl.pallas_call(
        kernel,
        out_shape=(jax.ShapeDtypeStruct(first_moment.shape, jnp.float32),) * 2,
        grid=(rows // tile,),
        in_specs=[on_chip()] * (len(projected) + 2),
        out_specs=(block, block),
        cost_estimate=pl.CostEstimate(flops=0, transcendentals=0, bytes_accessed=6 << 20),
        compiler_params=pltpu.CompilerParams(vmem_limit_bytes=SCRATCH_BYTES),
        name="new_moments",
    )(*kept_on_chip([*projected, first_moment, second_moment]))


def write_update(here, basis, chunks, places, update, all_columns):
    depth, rank = basis.shape
    cols = sum(row[0].shape[0] for row in chunks[0])
    flat = [stream for chunk in chunks for row in chunk for stream in row]
    held = () if update is None else (update,)
    n = all_columns // cols
    starts = range(0, cols, 256)
    blocks = [(low, min(256, cols - low)) for low in starts]

    def kernel(here_ref, base, *refs):
        out, made, sems = refs[-3:]
        left = list(refs[: len(flat)])
        copies = []
        for g, chunk in enumerate(chunks):
            rows = [[left.pop(0) for _ in row] for row in chunk]
            whole = jnp.concatenate(
                [jnp.concatenate([stream[...] for stream in row], axis=1) for row in rows], axis=0
            )
            column = chunk_at(here_ref, places[g], n) * cols
            for b, (low, size) in enumerate(blocks):
                made[g, :, low : low + size] = lax.dot_general(
                    base[...],
                    whole[low : low + size],
                    (((1,), (1,)), ((), ())),
                    preferred_element_type=jnp.float32,
                ).astype(made.dtype)
                columns = pl.ds(pl.multiple_of(column + low, 128), size)
                copy = pltpu.make_async_copy(
                    made.at[g, :, pl.ds(low, size)], out.at[:, columns], sems.at[g, b]
                )
                copy.start()
                copies.append(copy)
        for copy in copies:
            copy.wait()

    return pl.pallas_call(
        kernel,
        out_shape=jax.ShapeDtypeStruct((depth, all_columns), jnp.bfloat16),
        in_specs=[
            scalars(),
            *[on_chip()] * (1 + len(flat)),
            *[pl.BlockSpec(memory_space=pl.ANY)] * len(held),
        ],
        out_specs=pl.BlockSpec(memory_space=pl.ANY),
        scratch_shapes=[
            pltpu.VMEM((len(chunks), depth, cols), jnp.bfloat16),
            pltpu.SemaphoreType.DMA((len(chunks), len(blocks))),
        ],
        input_output_aliases={2 + len(flat): 0} if held else {},
        cost_estimate=pl.CostEstimate(
            flops=2 * depth * cols * rank * len(chunks),
            transcendentals=0,
            bytes_accessed=2 * depth * cols * len(chunks),
        ),
        compiler_params=pltpu.CompilerParams(vmem_limit_bytes=SCRATCH_BYTES),
        name="write_update",
    )(here, *kept_on_chip([basis, *flat]), *held)


def on_ring(n, m, activations, grad_out, basis, first_moment, second_moment):
    order = ring_order(n)
    upward = [(order[k], order[(k + 1) % n]) for k in range(n)]
    downward = [(b, a) for a, b in upward]
    partners = [(k, k ^ 1) for k in range(m)]

    def hop(to_up, to_down):
        return (lax.ppermute(to_up, "dp", upward), lax.ppermute(to_down, "dp", downward))

    me = lax.axis_index("mp")
    here, me, activations, basis = lax.optimization_barrier(
        (lax.axis_index("dp").reshape(1), me.reshape(1), activations, basis)
    )

    depth, _ = basis.shape
    all_columns = grad_out.shape[1]
    cols = all_columns // n
    half = n // 2
    streams = range(STREAMS)

    apart = [
        (a * m + k, b * m + k) for k in range(m) for a, b in (downward if k % 2 else upward)
    ]
    part = depth // 2
    passing = list(own_pieces(basis))
    pieces = [[(passing[s], 0, part)] for s in streams]
    kept, sent, far = split_columns(here, me, activations, n)
    swapped = lax.ppermute(sent, "mp", partners)
    fars = [far, lax.ppermute(far, "mp", partners)]
    for k in range(2, m, 2):
        far = lax.ppermute(fars[0], "mp", [(a, (a + k) % m) for a in range(m)])
        fars += [far, lax.ppermute(far, "mp", partners)]
    total = [None] * STREAMS
    for k in range(1, half):
        for s in streams:
            if k == half - 1:
                total[s] = add_coords(me, kept, swapped, None, pieces[s])
                pieces[s] = []
            passing[s] = lax.ppermute(passing[s], ("dp", "mp"), apart)
            pieces[s].append((passing[s], part + (k - 1) * depth, depth))

    coords, ups, downs = [None] * STREAMS, [None] * STREAMS, [None] * STREAMS
    for s in streams:
        near = add_coords(me, kept, swapped, total[s], pieces[s])
        sums = [near + lax.ppermute(near, "mp", partners)]
        sums += [lax.ppermute(sums[0], "mp", [(a, (a + k) % m) for a in range(m)]) for k in range(2, m, 2)]
        last = half_rows(me, passing[s])
        last = lax.ppermute(last, ("dp", "mp"), apart)
        lasts = [last, lax.ppermute(last, "mp", partners)]
        coords[s], ups[s], downs[s] = first_partials(here, me, grad_out, sums, fars, lasts, n, m)
        ups[s], downs[s] = hop(ups[s], downs[s])
    for k in range(2, half + 1):
        for s in streams:
            ups[s], downs[s] = [
                next_partials(here, grad_out, coords[s], came, n, half + 1 - k, way == "up")
                for way, came in (("up", ups[s]), ("down", downs[s]))
            ]
            ups[s], downs[s] = hop(ups[s], downs[s])
    projected = [None] * STREAMS
    direction = [None] * STREAMS
    for s in streams:
        projected[s], direction[s] = own_direction(
            here, grad_out, coords[s], ups[s], downs[s], first_moment, second_moment, s, n,
        )

    ups, downs = list(direction), list(direction)
    update = write_update(here, basis, [[direction]], [0], None, all_columns)
    first_new, second_new = new_moments(projected, first_moment, second_moment)
    for k in range(1, half):
        for s in streams:
            ups[s], downs[s] = hop(ups[s], downs[s])
        update = write_update(here, basis, [[list(ups)], [list(downs)]], [n - k, k], update, all_columns)
    for s in streams:
        ups[s], downs[s] = hop(ups[s][: cols // 2], downs[s][cols // 2 :])
    update = write_update(here, basis, [[ups, downs]], [half], update, all_columns)
    return (update, first_new, second_new)


def solution(mesh):
    n, m = mesh.shape["dp"], mesh.shape["mp"]
    ring = 6 <= n <= LONGEST_RING and n % 2 == 0 and m % 2 == 0
    placed = (
        P(("dp", "mp"), None),
        P("dp", "mp"),
        P("dp", None),
        P(("mp", "dp"), None),
        P(("mp", "dp"), None),
    )
    return jax.shard_map(
        functools.partial(on_ring, n, m) if ring else with_collectives,
        mesh=mesh,
        in_specs=placed,
        out_specs=(P("dp", "mp"), P(("mp", "dp"), None), P(("mp", "dp"), None)),
        check_vma=False,
    )
```

```python
import functools

import jax
import jax.numpy as jnp
from jax import lax
from jax.experimental import pallas as pl
from jax.experimental.pallas import tpu as pltpu
from jax.sharding import PartitionSpec as P

STEP = 1000


beta_first = 0.9
beta_second = 0.999
adam_eps = 1e-08

STREAMS = 2
WAYS = ("up", "down")
LONGEST_RING = 16
SCRATCH_BYTES = 12 << 20


def adam(projected, first_moment, second_moment):
    first_new = beta_first * first_moment + (1.0 - beta_first) * projected
    second_new = beta_second * second_moment + (1.0 - beta_second) * projected * projected
    corr_first = 1.0 - beta_first**STEP
    corr_second = 1.0 - beta_second**STEP
    direction = (first_new / corr_first / (jnp.sqrt(second_new / corr_second) + adam_eps)).astype(
        jnp.bfloat16
    )
    return first_new, second_new, direction


def with_collectives(activations, grad_out, basis, first_moment, second_moment):
    own_coords = jnp.dot(
        activations, lax.all_gather(basis, "dp", axis=0, tiled=True), preferred_element_type=jnp.float32
    ).astype(jnp.bfloat16)
    coords = lax.all_gather(own_coords, "mp", axis=0, tiled=True)
    projected = lax.psum_scatter(
        lax.dot_general(
            grad_out, coords, (((0,), (0,)), ((), ())), preferred_element_type=jnp.float32
        ),
        "dp",
        scatter_dimension=0,
        tiled=True,
    )
    first_new, second_new, direction = adam(projected, first_moment, second_moment)
    update = lax.dot_general(
        basis,
        lax.all_gather(direction, "dp", axis=0, tiled=True),
        (((1,), (1,)), ((), ())),
        preferred_element_type=jnp.float32,
    ).astype(jnp.bfloat16)
    return (update, first_new, second_new)


def on_chip():
    return pl.BlockSpec(memory_space=pltpu.VMEM)


def scalars():
    return pl.BlockSpec(memory_space=pltpu.SMEM)


def left_in_hbm(array):
    return pltpu.with_memory_space_constraint(array, pltpu.HBM)


def ring_order(n):
    return [*range(0, n, 2), *range(n - 1, 0, -2)]


def own_at(here, n):
    return lax.rem(here[0], n)


def chunk_at(here, away, n):
    index = own_at(here, n)
    step = lax.shift_right_logical(index, 1)
    place = lax.select(lax.bitwise_and(index, 1) == 0, step, n - 1 - step)
    there = lax.rem(place + lax.select(here[0] < n, away, n - away), n)
    return lax.select(there < n // 2, 2 * there, 2 * (n - 1 - there) + 1)


def kept_on_chip(arrays):
    return [pltpu.with_memory_space_constraint(a, pltpu.VMEM) for a in arrays]


def nearer_columns(here, me, activations, n, own, with_farthest):
    tokens, features = activations.shape
    depth = features // n
    part = depth // 2
    shapes = [part + (n // 2 - 1) * depth] + [depth] * with_farthest

    def kernel(here_ref, me_ref, source, *refs):
        out, sems = refs[0], refs[-1]
        side = lax.bitwise_xor(lax.bitwise_and(me_ref[0], 1), 0 if own else 1)
        copies = []

        def copy(start, size, out, low):
            columns = pl.ds(pl.multiple_of(start, 128), size)
            copies.append(
                pltpu.make_async_copy(source.at[:, columns], out.at[:, pl.ds(low, size)], sems.at[len(copies)])
            )

        copy(own_at(here_ref, n) * depth + side * part, part, out, 0)
        for k in range(1, n // 2):
            copy(chunk_at(here_ref, n - k if own else k, n) * depth, depth, out, part + (k - 1) * depth)
        if with_farthest:
            copy(chunk_at(here_ref, n // 2, n) * depth, depth, refs[1], 0)
        for one in copies:
            one.start()
        for one in copies:
            one.wait()

    return pl.pallas_call(
        kernel,
        out_shape=tuple(pltpu.VMEM((tokens, size), activations.dtype) for size in shapes),
        in_specs=[scalars(), scalars(), pl.BlockSpec(memory_space=pltpu.HBM)],
        out_specs=(on_chip(),) * len(shapes),
        scratch_shapes=[pltpu.SemaphoreType.DMA((n // 2 + with_farthest,))],
        compiler_params=pltpu.CompilerParams(vmem_limit_bytes=SCRATCH_BYTES),
    )(here, me, left_in_hbm(activations))


def own_piece(basis, s):
    depth, rank = basis.shape
    width = rank // STREAMS

    def kernel(source, out, sem):
        copy = pltpu.make_async_copy(source.at[:, pl.ds(s * width, width)], out, sem)
        copy.start()
        copy.wait()

    return pl.pallas_call(
        kernel,
        out_shape=pltpu.VMEM((depth, width), basis.dtype),
        in_specs=[pl.BlockSpec(memory_space=pltpu.HBM)],
        out_specs=on_chip(),
        scratch_shapes=[pltpu.SemaphoreType.DMA],
        compiler_params=pltpu.CompilerParams(vmem_limit_bytes=SCRATCH_BYTES),
    )(left_in_hbm(basis))


def half_rows(me, block):
    part = block.shape[0] // 2

    def kernel(me_ref, source, out):
        out[...] = source[pl.ds(pl.multiple_of(lax.bitwise_and(me_ref[0], 1) * part, part), part)]

    return pl.pallas_call(
        kernel,
        out_shape=pltpu.VMEM((part, block.shape[1]), block.dtype),
        in_specs=[scalars(), on_chip()],
        out_specs=on_chip(),
        compiler_params=pltpu.CompilerParams(vmem_limit_bytes=SCRATCH_BYTES),
    )(me, *kept_on_chip([block]))


def add_coords(me, kept, came, total, pieces):
    tokens, width = kept.shape[0], pieces[0][0].shape[1]
    held = () if total is None else (total,)
    arrays = [piece for piece, _, _ in pieces]

    def kernel(me_ref, *refs):
        out = refs[-1]
        side = lax.bitwise_and(me_ref[0], 1)
        refs_of = refs[2 + len(held) : -1]
        for act, place in ((refs[0], side), (refs[1], 1 - side)):
            rows = pl.ds(pl.multiple_of(place * tokens, tokens), tokens)
            acc = refs[2][rows] if held else jnp.zeros((tokens, width), jnp.float32)
            for ref, (_, low, size) in zip(refs_of, pieces, strict=True):
                own = pl.ds(pl.multiple_of(side * size, size), size) if size < ref.shape[0] else slice(None)
                acc += jnp.dot(act[:, low : low + size], ref[own], preferred_element_type=jnp.float32)
            out[rows] = acc

    return pl.pallas_call(
        kernel,
        out_shape=pltpu.VMEM((2 * tokens, width), jnp.float32),
        in_specs=[scalars(), *[on_chip()] * (2 + len(held) + len(arrays))],
        out_specs=on_chip(),
        cost_estimate=pl.CostEstimate(
            flops=4 * tokens * width * sum(size for _, _, size in pieces), transcendentals=0, bytes_accessed=4 << 20
        ),
        compiler_params=pltpu.CompilerParams(vmem_limit_bytes=SCRATCH_BYTES),
    )(me, *kept_on_chip([kept, came, *held, *arrays]))


def contract_tokens(grad, coords):
    return lax.dot_general(grad, coords, (((0,), (0,)), ((), ())), preferred_element_type=jnp.float32)


def first_partials(here, me, grad_out, sums, fars, lasts, n, m):
    group, width = sums[0].shape
    tokens, all_columns = grad_out.shape
    own_tokens = group // 2
    cols = all_columns // n
    part = lasts[0].shape[0]

    def kernel(here_ref, me_ref, grad, *refs):
        coords, top, bottom = refs[-3:]
        own_last, other_last = refs[-5:-3]
        side = lax.bitwise_and(me_ref[0], 1)
        own_columns = pl.ds(pl.multiple_of(side * part, part), part)
        other_columns = pl.ds(pl.multiple_of((1 - side) * part, part), part)
        for k, pair in enumerate(refs[: len(sums)]):
            first = lax.rem(lax.bitwise_and(me_ref[0], ~1) + m - 2 * k, m)
            for place, far in zip((side, 1 - side), refs[len(sums) + 2 * k :][:2], strict=True):
                total = (
                    pair[pl.ds(pl.multiple_of(place * own_tokens, own_tokens), own_tokens)]
                    + jnp.dot(far[:, own_columns], own_last[...], preferred_element_type=jnp.float32)
                    + jnp.dot(far[:, other_columns], other_last[...], preferred_element_type=jnp.float32)
                )
                low = pl.multiple_of((first + place) * own_tokens, own_tokens)
                coords[pl.ds(low, own_tokens)] = total.astype(jnp.bfloat16)
        column = pl.multiple_of(chunk_at(here_ref, n // 2, n) * cols, 128)
        sent = contract_tokens(grad[:, pl.ds(column, cols)], coords[...]).astype(jnp.bfloat16)
        top[...] = sent[: cols // 2]
        bottom[...] = sent[cols // 2 :]

    half = pltpu.VMEM((cols // 2, width), jnp.bfloat16)
    arrays = [grad_out, *sums, *fars, *lasts]
    return pl.pallas_call(
        kernel,
        out_shape=(pltpu.VMEM((tokens, width), jnp.bfloat16), half, half),
        in_specs=[scalars(), scalars(), *[on_chip()] * len(arrays)],
        out_specs=(on_chip(),) * 3,
        cost_estimate=pl.CostEstimate(
            flops=2 * tokens * (cols + 2 * part) * width, transcendentals=0, bytes_accessed=4 << 20
        ),
        compiler_params=pltpu.CompilerParams(vmem_limit_bytes=SCRATCH_BYTES),
    )(here, me, *kept_on_chip(arrays))


def next_partials(here, grad_out, coords, came, n, away, upward):
    tokens, width = coords.shape
    cols = grad_out.shape[1] // n
    rows = came.shape[0]
    added = slice(0, rows) if upward else slice(cols - rows, cols)
    rest = slice(rows, cols) if upward else slice(0, cols - rows)

    def kernel(here_ref, grad, coord, arrived, out):
        column = pl.multiple_of(chunk_at(here_ref, away if upward else n - away, n) * cols, 128)
        part = contract_tokens(grad[:, pl.ds(column, cols)], coord[...])
        out[added] = (part[added] + arrived[...].astype(jnp.float32)).astype(jnp.bfloat16)
        if rows < cols:
            out[rest] = part[rest].astype(jnp.bfloat16)

    return pl.pallas_call(
        kernel,
        out_shape=pltpu.VMEM((cols, width), jnp.bfloat16),
        in_specs=[scalars(), *[on_chip()] * 3],
        out_specs=on_chip(),
        cost_estimate=pl.CostEstimate(
            flops=2 * tokens * cols * width, transcendentals=0, bytes_accessed=2 << 20
        ),
        compiler_params=pltpu.CompilerParams(vmem_limit_bytes=SCRATCH_BYTES),
    )(here, *kept_on_chip([grad_out, coords, came]))


def own_direction(here, grad_out, coords, came_up, came_down, first_moment, second_moment, s, n):
    tokens, width = coords.shape
    cols = grad_out.shape[1] // n

    def kernel(here_ref, grad, coord, in_up, in_down, first, second, projected, direction):
        column = pl.multiple_of(own_at(here_ref, n) * cols, 128)
        total = (
            contract_tokens(grad[:, pl.ds(column, cols)], coord[...])
            + in_up[...].astype(jnp.float32)
            + in_down[...].astype(jnp.float32)
        )
        projected[...] = total
        mine = slice(s * width, (s + 1) * width)
        direction[...] = adam(total, first[:, mine], second[:, mine])[2]

    return pl.pallas_call(
        kernel,
        out_shape=(
            pltpu.VMEM((cols, width), jnp.float32),
            pltpu.VMEM((cols, width), jnp.bfloat16),
        ),
        in_specs=[scalars(), *[on_chip()] * 6],
        out_specs=(on_chip(),) * 2,
        cost_estimate=pl.CostEstimate(
            flops=2 * tokens * cols * width, transcendentals=0, bytes_accessed=4 << 20
        ),
        compiler_params=pltpu.CompilerParams(vmem_limit_bytes=SCRATCH_BYTES),
    )(here, *kept_on_chip([grad_out, coords, came_up, came_down, first_moment, second_moment]))


def new_moments(projected, first_moment, second_moment):
    width = projected[0].shape[1]
    rows = first_moment.shape[0]
    tile = rows // 2
    block = pl.BlockSpec((tile, first_moment.shape[1]), lambda r: (r, 0))

    def kernel(*refs):
        first, second, first_new, second_new = refs[len(projected) :]
        for s, ref in enumerate(refs[: len(projected)]):
            mine = slice(s * width, (s + 1) * width)
            at = pl.ds(pl.multiple_of(pl.program_id(0) * tile, tile), tile)
            first_new[:, mine], second_new[:, mine], _ = adam(ref[at], first[at, mine], second[at, mine])

    return pl.pallas_call(
        kernel,
        out_shape=(jax.ShapeDtypeStruct(first_moment.shape, jnp.float32),) * 2,
        grid=(rows // tile,),
        in_specs=[on_chip()] * (len(projected) + 2),
        out_specs=(block, block),
        cost_estimate=pl.CostEstimate(flops=0, transcendentals=0, bytes_accessed=6 << 20),
        compiler_params=pltpu.CompilerParams(vmem_limit_bytes=SCRATCH_BYTES),
    )(*kept_on_chip([*projected, first_moment, second_moment]))


def write_update(here, basis, chunks, places, update, all_columns):
    depth, rank = basis.shape
    cols = sum(row[0].shape[0] for row in chunks[0])
    flat = [stream for chunk in chunks for row in chunk for stream in row]
    held = () if update is None else (update,)
    n = all_columns // cols
    starts = range(0, cols, 256)
    blocks = [(low, min(256, cols - low)) for low in starts]

    def kernel(here_ref, base, *refs):
        out, made, sems = refs[-3:]
        left = list(refs[: len(flat)])
        copies = []
        for g, chunk in enumerate(chunks):
            rows = [[left.pop(0) for _ in row] for row in chunk]
            whole = jnp.concatenate(
                [jnp.concatenate([stream[...] for stream in row], axis=1) for row in rows], axis=0
            )
            column = chunk_at(here_ref, places[g], n) * cols
            for b, (low, size) in enumerate(blocks):
                made[g, :, low : low + size] = lax.dot_general(
                    base[...],
                    whole[low : low + size],
                    (((1,), (1,)), ((), ())),
                    preferred_element_type=jnp.float32,
                ).astype(made.dtype)
                columns = pl.ds(pl.multiple_of(column + low, 128), size)
                copy = pltpu.make_async_copy(
                    made.at[g, :, pl.ds(low, size)], out.at[:, columns], sems.at[g, b]
                )
                copy.start()
                copies.append(copy)
        for copy in copies:
            copy.wait()

    return pl.pallas_call(
        kernel,
        out_shape=jax.ShapeDtypeStruct((depth, all_columns), jnp.bfloat16),
        in_specs=[
            scalars(),
            *[on_chip()] * (1 + len(flat)),
            *[pl.BlockSpec(memory_space=pl.ANY)] * len(held),
        ],
        out_specs=pl.BlockSpec(memory_space=pl.ANY),
        scratch_shapes=[
            pltpu.VMEM((len(chunks), depth, cols), jnp.bfloat16),
            pltpu.SemaphoreType.DMA((len(chunks), len(blocks))),
        ],
        input_output_aliases={2 + len(flat): 0} if held else {},
        cost_estimate=pl.CostEstimate(
            flops=2 * depth * cols * rank * len(chunks),
            transcendentals=0,
            bytes_accessed=2 * depth * cols * len(chunks),
        ),
        compiler_params=pltpu.CompilerParams(vmem_limit_bytes=SCRATCH_BYTES),
    )(here, *kept_on_chip([basis, *flat]), *held)


def on_ring(n, m, activations, grad_out, basis, first_moment, second_moment):
    order = ring_order(n)
    ring = [(order[k], order[(k + 1) % n]) for k in range(n)]
    upward = [(b * m + k, a * m + k) if k % 2 else (a * m + k, b * m + k) for k in range(m) for a, b in ring]
    downward = [(b, a) for a, b in upward]
    partners = [(k, k ^ 1) for k in range(m)]

    def hop(to_up, to_down):
        return (lax.ppermute(to_up, ("dp", "mp"), upward), lax.ppermute(to_down, ("dp", "mp"), downward))

    me = lax.axis_index("mp")
    here, me, activations, basis = lax.optimization_barrier(
        ((lax.axis_index("dp") + n * lax.bitwise_and(me, 1)).reshape(1), me.reshape(1), activations, basis)
    )

    depth, _ = basis.shape
    all_columns = grad_out.shape[1]
    cols = all_columns // n
    half = n // 2
    streams = range(STREAMS)

    part = depth // 2
    passing = [own_piece(basis, s) for s in streams]
    pieces = [[(passing[s], 0, part)] for s in streams]
    (kept,) = nearer_columns(here, me, activations, n, True, False)
    sent, far = nearer_columns(here, me, activations, n, False, True)
    swapped = lax.ppermute(sent, "mp", partners)
    fars = [far, lax.ppermute(far, "mp", partners)]
    for k in range(2, m, 2):
        far = lax.ppermute(fars[0], "mp", [(a, (a + k) % m) for a in range(m)])
        fars += [far, lax.ppermute(far, "mp", partners)]
    total = [None] * STREAMS
    for k in range(1, half):
        for s in streams:
            if k == half - 1:
                total[s] = add_coords(me, kept, swapped, None, pieces[s])
                pieces[s] = []
            passing[s] = lax.ppermute(passing[s], ("dp", "mp"), upward)
            pieces[s].append((passing[s], part + (k - 1) * depth, depth))

    coords, ups, downs = [None] * STREAMS, [None] * STREAMS, [None] * STREAMS
    for s in streams:
        near = add_coords(me, kept, swapped, total[s], pieces[s])
        sums = [near + lax.ppermute(near, "mp", partners)]
        sums += [lax.ppermute(sums[0], "mp", [(a, (a + k) % m) for a in range(m)]) for k in range(2, m, 2)]
        last = half_rows(me, passing[s])
        last = lax.ppermute(last, ("dp", "mp"), upward)
        lasts = [last, lax.ppermute(last, "mp", partners)]
        coords[s], ups[s], downs[s] = first_partials(here, me, grad_out, sums, fars, lasts, n, m)
        ups[s], downs[s] = hop(ups[s], downs[s])
    for k in range(2, half + 1):
        for s in streams:
            ups[s], downs[s] = [
                next_partials(here, grad_out, coords[s], came, n, half + 1 - k, way == WAYS[0])
                for way, came in zip(WAYS, (ups[s], downs[s]), strict=True)
            ]
            ups[s], downs[s] = hop(ups[s], downs[s])
    projected = [None] * STREAMS
    direction = [None] * STREAMS
    for s in streams:
        projected[s], direction[s] = own_direction(
            here, grad_out, coords[s], ups[s], downs[s], first_moment, second_moment, s, n,
        )

    ups, downs = list(direction), list(direction)
    update = write_update(here, basis, [[direction]], [0], None, all_columns)
    first_new, second_new = new_moments(projected, first_moment, second_moment)
    for k in range(1, half):
        for s in streams:
            ups[s], downs[s] = hop(ups[s], downs[s])
        update = write_update(here, basis, [[list(ups)], [list(downs)]], [n - k, k], update, all_columns)
    for s in streams:
        ups[s], downs[s] = hop(ups[s][: cols // 2], downs[s][cols // 2 :])
    update = write_update(here, basis, [[ups, downs]], [half], update, all_columns)
    return (update, first_new, second_new)


def solution(mesh):
    n, m = mesh.shape["dp"], mesh.shape["mp"]
    ring = 6 <= n <= LONGEST_RING and n % 2 == 0 and m % 2 == 0
    placed = (
        P(("dp", "mp"), None),
        P("dp", "mp"),
        P("dp", None),
        P(("mp", "dp"), None),
        P(("mp", "dp"), None),
    )
    return jax.shard_map(
        functools.partial(on_ring, n, m) if ring else with_collectives,
        mesh=mesh,
        in_specs=placed,
        out_specs=(P("dp", "mp"), P(("mp", "dp"), None), P(("mp", "dp"), None)),
        check_vma=False,
    )
```
